1024 devices in a mesh: seq: 4 (over x), row: 8 (over y, core), col: 32 (over z).
Axes of the slice: x: 4, y: 4, z: 32, core: 2. Of those that a mesh axis runs over, the one named last changes fastest.
Arguments:
- inputs: bfloat16 [8, 32, 64, 4096], P('row', 'seq', None, 'col'), may hold values from -8 to 8
- query_proj: bfloat16 [8, 32, 64, 4096], P('row', 'seq', None, 'col'), may hold values from -5 to 5
- key_proj: bfloat16 [8, 32, 64, 4096], P('row', 'seq', None, 'col'), may hold values from -5 to 5
- value_proj: bfloat16 [8, 32, 64, 4096], P('row', 'seq', None, 'col'), may hold values from -6 to 6
- depth_weight: bfloat16 [7, 7, 4096], P(None, None, 'col'), may hold values from -1.25 to 1.25
- depth_bias: bfloat16 [4096], P('col'), may hold values from -3 to 3
- norm_gain: bfloat16 [4096], replicated, may hold values from 0.099609375 to 1.8984375
- norm_bias: bfloat16 [4096], replicated, may hold values from -3 to 3
- expand_weight: bfloat16 [4096, 16384], P(('seq', 'row'), 'col'), may hold values from -0.09375 to 0.09375
- expand_bias: bfloat16 [16384], P('col'), may hold values from -3 to 3
Outputs:
- residual_out: bfloat16 [8, 32, 64, 4096], P('row', 'seq', None, 'col')
- hidden: bfloat16 [8, 32, 64, 16384], P('row', 'seq', None, 'col')
The draws below stay inside these ranges and needn't reach their ends.
All inputs are finite; a program needn't handle non-finite values.
Results may differ from the reference program's by a relative error of at most 0.0075.
Values may be sent and summed in bfloat16 or wider, within the bound.
No kernel may reach another device: no remote copies, remote signals or barrier semaphores. Data moves between devices by JAX's collectives and lax.ppermute only.
A program may use at most 32 MiB of HBM per device.

```python
import math
import jax
import jax.numpy as jnp
from jax import lax

C = 4096
FF = 16384
HEAD_DIM = 128
KERNEL = 7
IMG_W = 64
HEADS = 32
IMG_H = 32
BATCH = 8


def draw_inputs(key, part):
    scale_key = jax.random.fold_in(key, 21)
    value_key = jax.random.fold_in(key, 22)
    row_scale = jnp.exp(jax.random.uniform(scale_key, (BATCH, IMG_H, IMG_W, 1), jnp.float32, math.log(0.3), math.log(3.0)))
    values = row_scale * jax.random.normal(value_key, (BATCH, IMG_H, IMG_W, C), jnp.float32)
    return jnp.clip(values, -8.0, 8.0).astype(jnp.bfloat16)


def base_draw(key, marker):
    sub_key = jax.random.fold_in(key, marker)
    shaped = (BATCH, IMG_H * IMG_W, HEADS, HEAD_DIM)
    values = jnp.clip(1.41 * jax.random.normal(sub_key, shaped, jnp.float32), -5.0, 5.0)
    return values


def draw_query_proj(key, part):
    values = base_draw(key, 41)
    return values.reshape(BATCH, IMG_H, IMG_W, C).astype(jnp.bfloat16)


def draw_key_proj(key, part):
    values = base_draw(key, 42)
    return values.reshape(BATCH, IMG_H, IMG_W, C).astype(jnp.bfloat16)


def draw_depth_weight(key, part):
    scale_key = jax.random.fold_in(key, 51)
    value_key = jax.random.fold_in(key, 52)
    channel_scale = jnp.exp(jax.random.uniform(scale_key, (1, 1, C), jnp.float32, math.log(0.3), math.log(3.0)))
    values = jax.random.normal(value_key, (KERNEL, KERNEL, C), jnp.float32)
    return jnp.clip(values * channel_scale / KERNEL, -1.25, 1.25).astype(jnp.bfloat16)


def block_levels(own_key, extent, pieces, least, largest):
    level = 1.0
    for position, blocks in pieces:
        heights = jax.random.uniform(jax.random.fold_in(jax.random.fold_in(own_key, 6), position), (blocks,), jnp.float32, least / len(pieces), largest / len(pieces))
        level = level * jnp.repeat(jnp.exp(heights), extent[position] // blocks).reshape((-1,) + (1,) * (len(extent) - 1 - position))
    return level


def centred(rng, shape, scale, most, pieces=(), kind=jnp.bfloat16):
    array = scale * jax.random.normal(rng, shape, jnp.float32)
    if pieces:
        array = array * block_levels(rng, shape, pieces, -0.22, 0.18)
    return jnp.clip(array, -most, most).astype(kind)


def setup_inputs(seed: int = 0) -> dict:
    streams_of = jax.random.split(jax.random.key(seed), 11)
    inputs = draw_inputs(jax.random.fold_in(streams_of[10], 71), 0)
    query_proj = draw_query_proj(jax.random.fold_in(streams_of[10], 71), 0)
    key_proj = draw_key_proj(jax.random.fold_in(streams_of[10], 71), 0)
    value_proj = centred(streams_of[3], (BATCH, IMG_H, IMG_W, C), 1.0, 6.0, ((0, 8), (1, 4), (3, 32)))
    depth_weight = draw_depth_weight(jax.random.fold_in(streams_of[10], 71), 0)
    depth_bias = centred(streams_of[5], (C,), 0.5, 3.0, ((0, 32),))
    norm_gain = jnp.clip(1.0 + 0.18 * jax.random.normal(streams_of[6], (C,), jnp.float32), 0.099609375, 1.8984375).astype(jnp.bfloat16)
    norm_bias = centred(streams_of[7], (C,), 0.5, 3.0)
    expand_weight = centred(streams_of[8], (C, FF), C ** -0.5, 0.09375, ((0, 32), (1, 32)))
    expand_bias = centred(streams_of[9], (FF,), 0.5, 3.0, ((0, 32),))
    return dict(inputs=inputs, query_proj=query_proj, key_proj=key_proj, value_proj=value_proj, depth_weight=depth_weight, depth_bias=depth_bias, norm_gain=norm_gain, norm_bias=norm_bias, expand_weight=expand_weight, expand_bias=expand_bias)


def settle(values):
    return lax.optimization_barrier(values.astype(jnp.bfloat16))

def attend_sample(parts):
    queries, keys_in, values_in = parts
    scores = jnp.einsum('qhd,khd->hqk', queries.astype(jnp.float32), keys_in.astype(jnp.float32)) * (1.0 / math.sqrt(HEAD_DIM))
    peak = lax.optimization_barrier(jnp.max(scores, axis=-1, keepdims=True))
    weights = jnp.exp(scores - peak)
    total = lax.optimization_barrier(jnp.sum(weights, axis=-1))
    rounded = settle(weights).astype(jnp.float32)
    summed = jnp.einsum('hqk,khd->qhd', rounded, values_in.astype(jnp.float32))
    return summed / jnp.transpose(total)[:, :, None]

def reference(inputs, query_proj, key_proj, value_proj, depth_weight, depth_bias, norm_gain, norm_bias, expand_weight, expand_bias):
    positions = IMG_H * IMG_W
    shaped = (BATCH, positions, HEADS, HEAD_DIM)
    attended = lax.map(attend_sample, (query_proj.reshape(shaped), key_proj.reshape(shaped), value_proj.reshape(shaped)))
    attended = attended.reshape(BATCH, IMG_H, IMG_W, C)
    residual_out = (inputs.astype(jnp.float32) + attended).astype(jnp.bfloat16)
    margin = KERNEL // 2
    padded = jnp.pad(settle(residual_out).astype(jnp.float32), ((0, 0), (margin, margin), (margin, margin), (0, 0)))
    kernel_taps = depth_weight.astype(jnp.float32)
    convolved = jnp.zeros((BATCH, IMG_H, IMG_W, C), jnp.float32)
    for row_tap in range(KERNEL):
        for col_tap in range(KERNEL):
            convolved = convolved + padded[:, row_tap:row_tap + IMG_H, col_tap:col_tap + IMG_W, :] * kernel_taps[row_tap, col_tap]
    convolved = settle(convolved + depth_bias.astype(jnp.float32))
    widened = convolved.reshape(BATCH * positions, C).astype(jnp.float32)
    center = lax.optimization_barrier(jnp.mean(widened, axis=1, keepdims=True))
    spread = lax.optimization_barrier(jnp.mean((widened - center) * (widened - center), axis=1, keepdims=True))
    normed = ((widened - center) / jnp.sqrt(spread + 1e-06) * norm_gain.astype(jnp.float32) + norm_bias.astype(jnp.float32)).astype(jnp.bfloat16)
    project = jnp.dot(normed, expand_weight, preferred_element_type=jnp.float32)
    hidden = jax.nn.gelu(project + expand_bias.astype(jnp.float32), approximate=False).astype(jnp.bfloat16)
    return (residual_out, hidden.reshape(BATCH, IMG_H, IMG_W, FF))
```

```python
import functools
import math

import jax
import jax.numpy as jnp
from jax import lax
from jax.experimental import pallas as pl
from jax.experimental.pallas import tpu as pltpu
from jax.sharding import PartitionSpec as P

HEAD_DIM = 128
KERNEL = 7
MARGIN = KERNEL // 2
IMG_W = 64
ROWS = 8
POS = ROWS * IMG_W
EDGE = MARGIN * IMG_W
C = 4096
SEQ = 4
CLASSES = 8
LEFT = 8
F32 = jnp.float32
BF16 = jnp.bfloat16


def shift(array, axis, by):
    peers = lax.axis_size(axis)
    return lax.ppermute(array, axis, [(i, (i + by) % peers) for i in range(peers)])


def attend_kernel(place, q, k, v, x, above, below, far, taps, bias, res, conv, qs, xs, image):
    qs[0:EDGE] = above[2 * POS : 2 * POS + EDGE]
    qs[EDGE : EDGE + POS] = q[...]
    qs[EDGE + POS :] = below[2 * POS : 2 * POS + EDGE]
    xs[0:EDGE] = above[2 * POS + EDGE :]
    xs[EDGE : EDGE + POS] = x[...]
    xs[EDGE + POS :] = below[2 * POS + EDGE :]
    tall = ROWS + 2 * MARGIN
    blank = jnp.zeros((tall, 8, HEAD_DIM), F32)
    image[:, 0:LEFT, :] = blank
    image[:, LEFT + IMG_W : LEFT + IMG_W + 8, :] = blank
    keys = [k[...], above[0:POS], below[0:POS], far[0:POS]]
    values = [v[...], above[POS : 2 * POS], below[POS : 2 * POS], far[POS : 2 * POS]]
    to_log2 = math.log2(math.e) / math.sqrt(HEAD_DIM)
    tile = 2 * IMG_W
    for t in range(tall // 2):
        own = slice(t * tile, (t + 1) * tile)
        queries = qs[own]
        scores = [
            lax.dot_general(queries, key, (((1,), (1,)), ((), ())), preferred_element_type=F32)
            for key in keys
        ]
        peak = functools.reduce(jnp.maximum, scores)
        peak = jnp.max(peak, axis=1, keepdims=True)
        weights = [jnp.exp2((score - peak) * to_log2) for score in scores]
        total = jnp.sum(functools.reduce(jnp.add, weights), axis=1, keepdims=True)
        summed = functools.reduce(
            jnp.add,
            [
                jnp.dot(weight.astype(BF16), value, preferred_element_type=F32)
                for weight, value in zip(weights, values)
            ],
        )
        out = (xs[own].astype(F32) + summed / total).astype(BF16).astype(F32)
        image[2 * t : 2 * t + 2, LEFT : LEFT + IMG_W, :] = out.reshape(2, IMG_W, HEAD_DIM)

    @pl.when(place[0] == 0)
    def _():
        image[0:MARGIN] = jnp.zeros((MARGIN, IMG_W + 16, HEAD_DIM), F32)

    @pl.when(place[0] == SEQ - 1)
    def _():
        image[tall - MARGIN :] = jnp.zeros((MARGIN, IMG_W + 16, HEAD_DIM), F32)

    for i in range(ROWS):
        res[i * IMG_W : (i + 1) * IMG_W] = image[MARGIN + i, LEFT : LEFT + IMG_W, :].astype(BF16)
    wide = 16
    for c0 in range(0, IMG_W, wide):
        sums = [jnp.broadcast_to(bias[...], (wide, HEAD_DIM)) for _ in range(ROWS)]
        for b in range(KERNEL):
            start = LEFT - MARGIN + b + c0
            columns = [image[r, start : start + wide, :] for r in range(tall)]
            for a in range(KERNEL):
                tap = taps[a * KERNEL + b : a * KERNEL + b + 1, :]
                for i in range(ROWS):
                    sums[i] = sums[i] + columns[i + a] * tap
        for i in range(ROWS):
            conv[i * IMG_W + c0 : i * IMG_W + c0 + wide] = sums[i].astype(BF16)


def attend(place, q, k, v, x, above, below, far, taps, bias):
    out = jax.ShapeDtypeStruct((POS, HEAD_DIM), BF16)
    vmem = pl.BlockSpec(memory_space=pltpu.VMEM)
    flops = 4 * (POS + 2 * EDGE) * SEQ * POS * HEAD_DIM
    return pl.pallas_call(
        attend_kernel,
        out_shape=(out, out),
        in_specs=[pl.BlockSpec(memory_space=pltpu.SMEM)] + [vmem] * 9,
        out_specs=(vmem, vmem),
        scratch_shapes=[
            pltpu.VMEM((POS + 2 * EDGE, HEAD_DIM), BF16),
            pltpu.VMEM((POS + 2 * EDGE, HEAD_DIM), BF16),
            pltpu.VMEM((ROWS + 2 * MARGIN, IMG_W + 16, HEAD_DIM), F32),
        ],
        compiler_params=pltpu.CompilerParams(vmem_limit_bytes=32 << 20),
        cost_estimate=pl.CostEstimate(flops=flops, bytes_accessed=2 << 20, transcendentals=2 << 20),
        name="attend",
    )(place, q, k, v, x, above, below, far, taps, bias)


AUX = 16


def slab(weights, group):
    return jnp.concatenate([weights[j, group] for j in range(SEQ)], axis=0)


def add_stats(blocks, pivot, sum1, sum2, rows=64):
    for t in range(0, POS, rows):
        here = slice(t, t + rows)
        centre, one, two = pivot[here], sum1[here], sum2[here]
        for block in blocks:
            away = block[here].astype(F32) - centre
            one = one + away
            two = two + away * away
        sum1[here] = one
        sum2[here] = two


def first_kernel(place, *refs):
    parts, (weights, aux, acc, pivot, sum1, sum2) = refs[:7], refs[7:]
    lead = jnp.mean(parts[0][0].astype(F32), axis=1, keepdims=True)
    pivot[...] = jnp.broadcast_to(lead, (POS, HEAD_DIM))
    sum1[...] = jnp.zeros((POS, HEAD_DIM), F32)
    sum2[...] = jnp.zeros((POS, HEAD_DIM), F32)
    for n, (offset, part) in enumerate(zip((0, -1, 1, -2, 2, -3, 3), parts)):
        group = lax.rem(place[0] + offset + CLASSES, CLASSES)
        left = jnp.concatenate([part[j] for j in range(SEQ)], axis=1)
        left = jnp.concatenate([left, aux[group]], axis=0)
        product = jnp.dot(left, slab(weights, group), preferred_element_type=F32)
        if n == 0:
            acc[...] = product
        else:
            acc[...] += product
        add_stats([part.at[j] for j in range(SEQ)], pivot, sum1, sum2)


def first(place, parts, weights, aux):
    vmem = pl.BlockSpec(memory_space=pltpu.VMEM)
    hidden = weights.shape[-1]
    stat = jax.ShapeDtypeStruct((POS, HEAD_DIM), F32)
    return pl.pallas_call(
        first_kernel,
        out_shape=(jax.ShapeDtypeStruct((POS + AUX, hidden), F32), stat, stat, stat),
        in_specs=[pl.BlockSpec(memory_space=pltpu.SMEM)] + [vmem] * 9,
        out_specs=(vmem,) * 4,
        compiler_params=pltpu.CompilerParams(vmem_limit_bytes=40 << 20),
        cost_estimate=pl.CostEstimate(flops=2 << 30, bytes_accessed=9 << 20, transcendentals=0),
        name="first",
    )(place, *parts, weights, aux)


def last_kernel(place, acc, pivot, sum1, sum2, above, below, weights, aux, bias, out):
    group = lax.rem(place[0] + 4, CLASSES)
    blocks = [above.at[0], above.at[1], below.at[0], below.at[1]]
    left = jnp.concatenate([block[...] for block in blocks], axis=1)
    left = jnp.concatenate([left, aux[group]], axis=0)
    product = acc[...] + jnp.dot(left, slab(weights, group), preferred_element_type=F32)
    add_stats(blocks, pivot, sum1, sum2)
    mean1 = jnp.sum(sum1[...], axis=1, keepdims=True) * (1.0 / C)
    mean2 = jnp.sum(sum2[...], axis=1, keepdims=True) * (1.0 / C)
    centre = pivot[:, 0:1] + mean1
    spread = jnp.maximum(mean2 - mean1 * mean1, 0.0)
    scale = lax.rsqrt(spread + 1e-06)
    slope = product[POS : POS + 1]
    level = product[POS + 1 : POS + 2] + product[POS + 2 : POS + 3] + bias[...]
    project = scale * (product[0:POS] - centre * slope) + level
    out[...] = (0.5 * project * (1.0 + lax.erf(project * math.sqrt(0.5)))).astype(BF16)


def last(place, acc, stats, above, below, weights, aux, bias):
    vmem = pl.BlockSpec(memory_space=pltpu.VMEM)
    hidden = weights.shape[-1]
    return pl.pallas_call(
        last_kernel,
        out_shape=jax.ShapeDtypeStruct((POS, hidden), BF16),
        in_specs=[pl.BlockSpec(memory_space=pltpu.SMEM)] + [vmem] * 9,
        out_specs=vmem,
        compiler_params=pltpu.CompilerParams(vmem_limit_bytes=40 << 20),
        cost_estimate=pl.CostEstimate(flops=1 << 29, bytes_accessed=7 << 20, transcendentals=1 << 18),
        name="last",
    )(place, acc, *stats, above, below, weights, aux, bias)


def on_device(
    inputs,
    query_proj,
    key_proj,
    value_proj,
    depth_weight,
    depth_bias,
    norm_gain,
    norm_bias,
    expand_weight,
    expand_bias,
):
    seq, row, col = (lax.axis_index(axis) for axis in ("seq", "row", "col"))
    depth, hidden = expand_weight.shape
    gain, offset = norm_gain.astype(F32), norm_bias.astype(F32)
    my_gain = lax.dynamic_slice(gain, ((seq * CLASSES + row) * depth,), (depth,))
    scaled = (expand_weight.astype(F32) * my_gain[:, None]).astype(BF16)
    weights = lax.all_gather(scaled, ("seq", "row"), axis=0, tiled=True)
    weights = weights.reshape(SEQ, CLASSES, depth, hidden)
    ratio = offset / gain
    high = lax.reduce_precision(ratio, 8, 7)
    aux = jnp.stack([jnp.ones_like(ratio), high, ratio - high] + [jnp.zeros_like(ratio)] * (AUX - 3))
    aux = aux.astype(BF16).reshape(AUX, SEQ, CLASSES, depth)
    aux = jnp.transpose(aux, (2, 0, 1, 3)).reshape(CLASSES, AUX, SEQ * depth)

    x, q, k, v = (a.reshape(POS, HEAD_DIM) for a in (inputs, query_proj, key_proj, value_proj))
    both = jnp.concatenate([k, v])
    far = shift(both, "seq", 2)
    above = shift(jnp.concatenate([k, v, q[POS - EDGE :], x[POS - EDGE :]]), "seq", 1)
    below = shift(jnp.concatenate([k, v, q[:EDGE], x[:EDGE]]), "seq", -1)
    taps = depth_weight.astype(F32).reshape(KERNEL * KERNEL, HEAD_DIM)
    bias = depth_bias.astype(F32).reshape(1, HEAD_DIM)
    residual, convolved = attend(
        seq.astype(jnp.int32).reshape(1), q, k, v, x, above, below, far, taps, bias
    )

    strides = [[i + CLASSES * j for j in range(SEQ)] for i in range(CLASSES)]
    own = lax.all_gather(convolved, "col", axis=0, tiled=True, axis_index_groups=strides)
    own = own.reshape(SEQ, POS, HEAD_DIM)
    parts, up, down = [own], own, own
    for _ in range(3):
        up, down = shift(up, "col", 1), shift(down, "col", -1)
        parts += [up, down]
    up, down = shift(up[:2], "col", 1), shift(down[2:], "col", -1)
    place = col.astype(jnp.int32).reshape(1)
    acc, *stats = first(place, parts, weights, aux)
    out = last(
        place, acc, stats, up, down, weights, aux, expand_bias.astype(F32).reshape(1, hidden)
    )
    return (
        residual.reshape(inputs.shape),
        out.reshape(inputs.shape[:3] + (hidden,)),
    )


def solution(mesh):
    return jax.shard_map(
        on_device,
        mesh=mesh,
        in_specs=(
            P("row", "seq", None, "col"),
            P("row", "seq", None, "col"),
            P("row", "seq", None, "col"),
            P("row", "seq", None, "col"),
            P(None, None, "col"),
            P("col"),
            P(),
            P(),
            P(("seq", "row"), "col"),
            P("col"),
        ),
        out_specs=(P("row", "seq", None, "col"), P("row", "seq", None, "col")),
        check_vma=False,
    )
```

```python
import functools
import math

import jax
import jax.numpy as jnp
from jax import lax
from jax.experimental import pallas as pl
from jax.experimental.pallas import tpu as pltpu
from jax.sharding import PartitionSpec as P

HEAD_DIM = 128
KERNEL = 7
MARGIN = KERNEL // 2
IMG_W = 64
ROWS = 8
POS = ROWS * IMG_W
EDGE = MARGIN * IMG_W
C = 4096
SEQ = 4
CLASSES = 8
LEFT = 8
F32 = jnp.float32
BF16 = jnp.bfloat16


def shift(array, axis, by):
    peers = lax.axis_size(axis)
    return lax.ppermute(array, axis, [(i, (i + by) % peers) for i in range(peers)])


def pack_kernel(place, k, v, q, x, weight_in, gain_in, kv, lower, upper, scaled, weight, gain, sems):
    first, end = slice(0, EDGE), slice(POS - EDGE, POS)
    moves = [(weight_in, weight), (gain_in, gain), (k, kv.at[0:POS]), (v, kv.at[POS:])]
    for message, edge in ((lower, end), (upper, first)):
        moves += [
            (k, message.at[0:POS]),
            (v, message.at[POS : 2 * POS]),
            (q.at[edge], message.at[2 * POS : 2 * POS + EDGE]),
            (x.at[edge], message.at[2 * POS + EDGE :]),
        ]
    copies = [pltpu.make_async_copy(a, b, sems.at[i]) for i, (a, b) in enumerate(moves)]
    for copy in copies:
        copy.start()
    for copy in copies[:2]:
        copy.wait()
    depth = weight.shape[0]
    gains = gain[...].astype(F32)
    line = lax.broadcasted_iota(jnp.int32, gains.shape, 0) == place[0]
    mine = jnp.sum(jnp.where(line, gains, 0.0), axis=0, keepdims=True)
    mine = jnp.transpose(jnp.broadcast_to(mine, (depth, depth)))
    for c in range(0, weight.shape[1], depth):
        scaled[:, c : c + depth] = (weight[:, c : c + depth].astype(F32) * mine).astype(BF16)
    for copy in copies[2:]:
        copy.wait()


def pack(place, k, v, q, x, weight, gain):
    vmem, here = pl.BlockSpec(memory_space=pltpu.VMEM), pl.BlockSpec(memory_space=pltpu.HBM)
    two = jax.ShapeDtypeStruct((2 * POS, HEAD_DIM), BF16)
    message = jax.ShapeDtypeStruct((2 * (POS + EDGE), HEAD_DIM), BF16)
    return pl.pallas_call(
        pack_kernel,
        out_shape=(two, message, message, jax.ShapeDtypeStruct(weight.shape, BF16)),
        in_specs=[pl.BlockSpec(memory_space=pltpu.SMEM)] + [here] * 6,
        out_specs=(vmem,) * 4,
        scratch_shapes=[
            pltpu.VMEM(weight.shape, BF16),
            pltpu.VMEM(gain.shape, BF16),
            pltpu.SemaphoreType.DMA((12,)),
        ],
        compiler_params=pltpu.CompilerParams(vmem_limit_bytes=8 << 20),
        name="pack",
    )(place, k, v, q, x, weight, gain)


def attend_kernel(place, k, v, q, x, above, below, far, taps, bias, res, conv, kv, qs, xs, image, sems):
    middle = slice(EDGE, EDGE + POS)
    moves = ((k, kv.at[0:POS]), (v, kv.at[POS:]), (q, qs.at[middle]), (x, xs.at[middle]))
    copies = [pltpu.make_async_copy(a, b, sems.at[i]) for i, (a, b) in enumerate(moves)]
    for copy in copies:
        copy.start()
    qs[0:EDGE] = above[2 * POS : 2 * POS + EDGE]
    qs[EDGE + POS :] = below[2 * POS : 2 * POS + EDGE]
    xs[0:EDGE] = above[2 * POS + EDGE :]
    xs[EDGE + POS :] = below[2 * POS + EDGE :]
    tall = ROWS + 2 * MARGIN
    blank = jnp.zeros((tall, 8, HEAD_DIM), F32)
    image[:, 0:LEFT, :] = blank
    image[:, LEFT + IMG_W : LEFT + IMG_W + 8, :] = blank
    for copy in copies:
        copy.wait()
    keys = [part[0:POS] for part in (kv, above, below, far)]
    values = [part[POS : 2 * POS] for part in (kv, above, below, far)]
    to_log2 = math.log2(math.e) / math.sqrt(HEAD_DIM)
    tile = 2 * IMG_W
    for t in range(tall // 2):
        own = slice(t * tile, (t + 1) * tile)
        queries = qs[own]
        scores = [
            lax.dot_general(queries, key, (((1,), (1,)), ((), ())), preferred_element_type=F32)
            for key in keys
        ]
        peak = functools.reduce(jnp.maximum, scores)
        peak = jnp.max(peak, axis=1, keepdims=True)
        weights = [jnp.exp2((score - peak) * to_log2) for score in scores]
        total = jnp.sum(functools.reduce(jnp.add, weights), axis=1, keepdims=True)
        summed = functools.reduce(
            jnp.add,
            [
                jnp.dot(weight.astype(BF16), value, preferred_element_type=F32)
                for weight, value in zip(weights, values)
            ],
        )
        out = (xs[own].astype(F32) + summed / total).astype(BF16).astype(F32)
        image[2 * t : 2 * t + 2, LEFT : LEFT + IMG_W, :] = out.reshape(2, IMG_W, HEAD_DIM)

    @pl.when(place[0] == 0)
    def _():
        image[0:MARGIN] = jnp.zeros((MARGIN, IMG_W + 16, HEAD_DIM), F32)

    @pl.when(place[0] == SEQ - 1)
    def _():
        image[tall - MARGIN :] = jnp.zeros((MARGIN, IMG_W + 16, HEAD_DIM), F32)

    for i in range(ROWS):
        res[i * IMG_W : (i + 1) * IMG_W] = image[MARGIN + i, LEFT : LEFT + IMG_W, :].astype(BF16)
    wide = 16
    for c0 in range(0, IMG_W, wide):
        sums = [jnp.broadcast_to(bias[...], (wide, HEAD_DIM)) for _ in range(ROWS)]
        for b in range(KERNEL):
            start = LEFT - MARGIN + b + c0
            columns = [image[r, start : start + wide, :] for r in range(tall)]
            for a in range(KERNEL):
                tap = taps[a * KERNEL + b : a * KERNEL + b + 1, :]
                for i in range(ROWS):
                    sums[i] = sums[i] + columns[i + a] * tap
        for i in range(ROWS):
            conv[i * IMG_W + c0 : i * IMG_W + c0 + wide] = sums[i].astype(BF16)


def attend(place, k, v, q, x, above, below, far, taps, bias):
    out = jax.ShapeDtypeStruct((POS, HEAD_DIM), BF16)
    vmem, here = pl.BlockSpec(memory_space=pltpu.VMEM), pl.BlockSpec(memory_space=pltpu.HBM)
    flops = 4 * (POS + 2 * EDGE) * SEQ * POS * HEAD_DIM
    return pl.pallas_call(
        attend_kernel,
        out_shape=(out, out),
        in_specs=[pl.BlockSpec(memory_space=pltpu.SMEM)] + [here] * 4 + [vmem] * 5,
        out_specs=(vmem, vmem),
        scratch_shapes=[
            pltpu.VMEM((2 * POS, HEAD_DIM), BF16),
            pltpu.VMEM((POS + 2 * EDGE, HEAD_DIM), BF16),
            pltpu.VMEM((POS + 2 * EDGE, HEAD_DIM), BF16),
            pltpu.VMEM((ROWS + 2 * MARGIN, IMG_W + 16, HEAD_DIM), F32),
            pltpu.SemaphoreType.DMA((4,)),
        ],
        compiler_params=pltpu.CompilerParams(vmem_limit_bytes=16 << 20),
        cost_estimate=pl.CostEstimate(flops=flops, bytes_accessed=2 << 20, transcendentals=2 << 20),
        name="attend",
    )(place, k, v, q, x, above, below, far, taps, bias)


AUX = 16


def fetch(weights, groups, slabs, sems):
    copies = []
    for n, group in enumerate(groups):
        rows = weights.shape[2]
        copies.append(
            [
                pltpu.make_async_copy(
                    weights.at[j, group], slabs.at[n, j * rows : (j + 1) * rows], sems.at[n, j]
                )
                for j in range(SEQ)
            ]
        )
        for copy in copies[-1]:
            copy.start()
    return copies


def slab_scratch(count, weights):
    _, _, rows, columns = weights.shape
    return [
        pltpu.VMEM((count, SEQ * rows, columns), BF16),
        pltpu.SemaphoreType.DMA((count, SEQ)),
    ]


def extra_rows(gain, offset, group):
    tiles = []
    for j in range(SEQ):
        here = pl.ds(j * CLASSES + group, 1)
        ratio = offset[here] / gain[here]
        high = ratio.astype(BF16).astype(F32)
        row = lax.broadcasted_iota(jnp.int32, (AUX, HEAD_DIM), 0)
        tile = jnp.where(row == 0, 1.0, 0.0)
        tile = jnp.where(row == 1, jnp.broadcast_to(high, tile.shape), tile)
        tile = jnp.where(row == 2, jnp.broadcast_to(ratio - high, tile.shape), tile)
        tiles.append(tile.astype(BF16))
    return jnp.concatenate(tiles, axis=1)


def product_of(blocks, copies, slab, gain, offset, group):
    left = jnp.concatenate([block[...] for block in blocks], axis=1)
    left = jnp.concatenate([left, extra_rows(gain, offset, group)], axis=0)
    for copy in copies:
        copy.wait()
    return jnp.dot(left, slab[...], preferred_element_type=F32)


def add_stats(blocks, pivot, before1, before2, sum1, sum2, rows=64):
    for t in range(0, POS, rows):
        here = slice(t, t + rows)
        centre, one, two = pivot[here], before1[here], before2[here]
        for block in blocks:
            away = block[here].astype(F32) - centre
            one = one + away
            two = two + away * away
        sum1[here] = one
        sum2[here] = two


def first_kernel(offsets, place, *refs):
    count = len(offsets)
    parts, refs = refs[:count], refs[count:]
    weights, gain, offset, acc, pivot, sum1, sum2, slabs, sems = refs
    groups = [lax.rem(place[0] + away + CLASSES, CLASSES) for away in offsets]
    copies = fetch(weights, groups, slabs, sems)
    lead = jnp.mean(parts[0][0].astype(F32), axis=1, keepdims=True)
    pivot[...] = jnp.broadcast_to(lead, (POS, HEAD_DIM))
    sum1[...] = jnp.zeros((POS, HEAD_DIM), F32)
    sum2[...] = jnp.zeros((POS, HEAD_DIM), F32)
    for n, part in enumerate(parts):
        blocks = [part.at[j] for j in range(SEQ)]
        product = product_of(blocks, copies[n], slabs.at[n], gain, offset, groups[n])
        if n == 0:
            acc[...] = product
        else:
            acc[...] += product
        add_stats(blocks, pivot, sum1, sum2, sum1, sum2)


def more_kernel(offsets, place, *refs):
    count = len(offsets)
    parts, refs = refs[:count], refs[count:]
    acc, pivot, sum1, sum2, weights, gain, offset, acc_out, sum1_out, sum2_out, slabs, sems = refs
    groups = [lax.rem(place[0] + away + CLASSES, CLASSES) for away in offsets]
    copies = fetch(weights, groups, slabs, sems)
    for n, part in enumerate(parts):
        blocks = [part.at[j] for j in range(SEQ)]
        before = (acc, sum1, sum2) if n == 0 else (acc_out, sum1_out, sum2_out)
        product = product_of(blocks, copies[n], slabs.at[n], gain, offset, groups[n])
        acc_out[...] = before[0][...] + product
        add_stats(blocks, pivot, before[1], before[2], sum1_out, sum2_out)


def stage(kernel, offsets, place, parts, before, weights, gain, offset):
    vmem, here = pl.BlockSpec(memory_space=pltpu.VMEM), pl.BlockSpec(memory_space=pltpu.HBM)
    hidden = weights.shape[-1]
    stat = jax.ShapeDtypeStruct((POS, HEAD_DIM), F32)
    total = jax.ShapeDtypeStruct((POS + AUX, hidden), F32)
    out_shape = (total, stat, stat) if before else (total, stat, stat, stat)
    return pl.pallas_call(
        functools.partial(kernel, offsets),
        out_shape=out_shape,
        in_specs=[pl.BlockSpec(memory_space=pltpu.SMEM)]
        + [vmem] * (len(parts) + len(before))
        + [here, vmem, vmem],
        out_specs=(vmem,) * len(out_shape),
        scratch_shapes=slab_scratch(len(parts), weights),
        compiler_params=pltpu.CompilerParams(vmem_limit_bytes=16 << 20),
        cost_estimate=pl.CostEstimate(
            flops=len(parts) << 28, bytes_accessed=len(parts) << 20, transcendentals=0
        ),
        name="stage",
    )(place, *parts, *before, weights, gain, offset)


def last_kernel(place, *refs):
    acc, pivot, sum1, sum2, above, below, weights, gain, offset, bias, out, one, two, slabs, sems = refs
    group = lax.rem(place[0] + 4, CLASSES)
    (copies,) = fetch(weights, [group], slabs, sems)
    blocks = [above.at[0], above.at[1], below.at[0], below.at[1]]
    add_stats(blocks, pivot, sum1, sum2, one, two)
    product = acc[...] + product_of(blocks, copies, slabs.at[0], gain, offset, group)
    mean1 = jnp.sum(one[...], axis=1, keepdims=True) * (1.0 / C)
    mean2 = jnp.sum(two[...], axis=1, keepdims=True) * (1.0 / C)
    centre = pivot[:, 0:1] + mean1
    spread = jnp.maximum(mean2 - mean1 * mean1, 0.0)
    scale = lax.rsqrt(spread + 1e-06)
    slope = product[POS : POS + 1]
    level = product[POS + 1 : POS + 2] + product[POS + 2 : POS + 3] + bias[...]
    project = scale * (product[0:POS] - centre * slope) + level
    out[...] = (0.5 * project * (1.0 + lax.erf(project * math.sqrt(0.5)))).astype(BF16)


def last(place, acc, stats, above, below, weights, gain, offset, bias):
    vmem, here = pl.BlockSpec(memory_space=pltpu.VMEM), pl.BlockSpec(memory_space=pltpu.HBM)
    hidden = weights.shape[-1]
    return pl.pallas_call(
        last_kernel,
        out_shape=jax.ShapeDtypeStruct((POS, hidden), BF16),
        in_specs=[pl.BlockSpec(memory_space=pltpu.SMEM)] + [vmem] * 6 + [here] + [vmem] * 3,
        out_specs=vmem,
        scratch_shapes=[pltpu.VMEM((POS, HEAD_DIM), F32)] * 2 + slab_scratch(1, weights),
        compiler_params=pltpu.CompilerParams(vmem_limit_bytes=16 << 20),
        cost_estimate=pl.CostEstimate(flops=1 << 28, bytes_accessed=7 << 20, transcendentals=1 << 18),
        name="last",
    )(place, acc, *stats, above, below, weights, gain, offset, bias)


def on_device(
    inputs,
    query_proj,
    key_proj,
    value_proj,
    depth_weight,
    depth_bias,
    norm_gain,
    norm_bias,
    expand_weight,
    expand_bias,
):
    seq, row, col = (lax.axis_index(axis) for axis in ("seq", "row", "col"))
    depth, hidden = expand_weight.shape
    gain, offset = (a.reshape(C // depth, depth) for a in (norm_gain, norm_bias))
    x, q, k, v = (a.reshape(POS, HEAD_DIM) for a in (inputs, query_proj, key_proj, value_proj))
    x, q, k, v = (pltpu.with_memory_space_constraint(a, pltpu.HBM) for a in (x, q, k, v))
    mine = (seq * CLASSES + row).astype(jnp.int32).reshape(1)
    held = (pltpu.with_memory_space_constraint(a, pltpu.HBM) for a in (expand_weight, gain))
    kv, lower, upper, scaled = pack(mine, k, v, q, x, *held)
    far = shift(kv, "seq", 2)
    above, below = shift(lower, "seq", 1), shift(upper, "seq", -1)
    weights = lax.all_gather(scaled, ("seq", "row"), axis=0, tiled=True)
    weights = weights.reshape(SEQ, CLASSES, depth, hidden)
    weights = pltpu.with_memory_space_constraint(weights, pltpu.HBM)
    gain, offset = gain.astype(F32), offset.astype(F32)
    taps = depth_weight.astype(F32).reshape(KERNEL * KERNEL, HEAD_DIM)
    bias = depth_bias.astype(F32).reshape(1, HEAD_DIM)
    residual, convolved = attend(
        seq.astype(jnp.int32).reshape(1), k, v, q, x, above, below, far, taps, bias
    )

    strides = [[i + CLASSES * j for j in range(SEQ)] for i in range(CLASSES)]
    own = lax.all_gather(convolved, "col", axis=0, tiled=True, axis_index_groups=strides)
    own = own.reshape(SEQ, POS, HEAD_DIM)
    pairs, up, down = [], own, own
    for _ in range(3):
        up, down = shift(up, "col", 1), shift(down, "col", -1)
        pairs.append((up, down))
    place = col.astype(jnp.int32).reshape(1)
    parts = (own, *pairs[0], *pairs[1])
    before = stage(first_kernel, (0, -1, 1, -2, 2), place, parts, (), weights, gain, offset)
    up, down, before = lax.optimization_barrier((up, down, before))
    pairs[2] = (up, down)
    up, down = shift(up[:2], "col", 1), shift(down[2:], "col", -1)
    acc, *sums = stage(more_kernel, (-3, 3), place, pairs[2], before, weights, gain, offset)
    pivot = before[1]
    bias = expand_bias.astype(F32).reshape(1, hidden)
    out = last(place, acc, (pivot, *sums), up, down, weights, gain, offset, bias)
    return (
        residual.reshape(inputs.shape),
        out.reshape(inputs.shape[:3] + (hidden,)),
    )


def solution(mesh):
    return jax.shard_map(
        on_device,
        mesh=mesh,
        in_specs=(
            P("row", "seq", None, "col"),
            P("row", "seq", None, "col"),
            P("row", "seq", None, "col"),
            P("row", "seq", None, "col"),
            P(None, None, "col"),
            P("col"),
            P(),
            P(),
            P(("seq", "row"), "col"),
            P("col"),
        ),
        out_specs=(P("row", "seq", None, "col"), P("row", "seq", None, "col")),
        check_vma=False,
    )
```

```python
import functools
import math

import jax
import jax.numpy as jnp
from jax import lax
from jax.experimental import pallas as pl
from jax.experimental.pallas import tpu as pltpu
from jax.sharding import PartitionSpec as P

HEAD_DIM = 128
KERNEL = 7
MARGIN = KERNEL // 2
IMG_W = 64
ROWS = 8
POS = ROWS * IMG_W
EDGE = MARGIN * IMG_W
C = 4096
SEQ = 4
CLASSES = 8
LEFT = 8
F32 = jnp.float32
BF16 = jnp.bfloat16


def shift(array, axis, by):
    peers = lax.axis_size(axis)
    return lax.ppermute(array, axis, [(i, (i + by) % peers) for i in range(peers)])


def move(pairs, sems):
    copies = [pltpu.make_async_copy(a, b, sems.at[i]) for i, (a, b) in enumerate(pairs)]
    for copy in copies:
        copy.start()
    return copies


def message_moves(k, v, q, x, message, edge):
    return [
        (k, message.at[0:POS]),
        (v, message.at[POS : 2 * POS]),
        (q.at[edge], message.at[2 * POS : 2 * POS + EDGE]),
        (x.at[edge], message.at[2 * POS + EDGE :]),
    ]


def pack_kernel(k, v, q, x, qx, lower, sems):
    own = [(q, qx.at[0:POS]), (x, qx.at[POS:])]
    edge = slice(POS - EDGE, POS)
    for copy in move(own + message_moves(k, v, q, x, lower, edge), sems):
        copy.wait()


def pack(k, v, q, x):
    vmem, here = pl.BlockSpec(memory_space=pltpu.VMEM), pl.BlockSpec(memory_space=pltpu.HBM)
    two = jax.ShapeDtypeStruct((2 * POS, HEAD_DIM), BF16)
    message = jax.ShapeDtypeStruct((2 * (POS + EDGE), HEAD_DIM), BF16)
    return pl.pallas_call(
        pack_kernel,
        out_shape=(two, message),
        in_specs=[here] * 4,
        out_specs=(vmem,) * 2,
        scratch_shapes=[pltpu.SemaphoreType.DMA((6,))],
        compiler_params=pltpu.CompilerParams(vmem_limit_bytes=8 << 20),
        name="pack",
    )(k, v, q, x)


def scale_kernel(place, k, v, q, x, weight_in, gain_in, kv, upper, scaled, weight, gain, sems):
    pairs = [(weight_in, weight), (gain_in, gain), (k, kv.at[0:POS]), (v, kv.at[POS:])]
    copies = move(pairs + message_moves(k, v, q, x, upper, slice(0, EDGE)), sems)
    for copy in copies[:2]:
        copy.wait()
    depth = weight.shape[0]
    gains = gain[...].astype(F32)
    line = lax.broadcasted_iota(jnp.int32, gains.shape, 0) == place[0]
    mine = jnp.sum(jnp.where(line, gains, 0.0), axis=0, keepdims=True)
    mine = jnp.transpose(jnp.broadcast_to(mine, (depth, depth)))
    for c in range(0, weight.shape[1], depth):
        scaled[:, c : c + depth] = (weight[:, c : c + depth].astype(F32) * mine).astype(BF16)
    for copy in copies[2:]:
        copy.wait()


def scale(place, k, v, q, x, weight, gain):
    vmem, here = pl.BlockSpec(memory_space=pltpu.VMEM), pl.BlockSpec(memory_space=pltpu.HBM)
    message = jax.ShapeDtypeStruct((2 * (POS + EDGE), HEAD_DIM), BF16)
    return pl.pallas_call(
        scale_kernel,
        out_shape=(
            jax.ShapeDtypeStruct((2 * POS, HEAD_DIM), BF16),
            message,
            jax.ShapeDtypeStruct(weight.shape, BF16),
        ),
        in_specs=[pl.BlockSpec(memory_space=pltpu.SMEM)] + [here] * 6,
        out_specs=(vmem,) * 3,
        scratch_shapes=[
            pltpu.VMEM(weight.shape, BF16),
            pltpu.VMEM(gain.shape, BF16),
            pltpu.SemaphoreType.DMA((8,)),
        ],
        compiler_params=pltpu.CompilerParams(vmem_limit_bytes=8 << 20),
        name="scale",
    )(place, k, v, q, x, weight, gain)


def join_kernel(*refs):
    *refs, out, sems = refs
    count = len(refs)
    copies = [pltpu.make_async_copy(refs[i], out.at[i], sems.at[i]) for i in range(count)]
    for copy in copies:
        copy.start()
    for copy in copies:
        copy.wait()


def join(parts):
    count, here = len(parts), pl.BlockSpec(memory_space=pltpu.HBM)
    shape = (count,) + parts[0].shape
    parts = [pltpu.with_memory_space_constraint(part, pltpu.HBM) for part in parts]
    return pl.pallas_call(
        join_kernel,
        out_shape=pltpu.HBM(shape, BF16),
        in_specs=[here] * count,
        out_specs=here,
        scratch_shapes=[pltpu.SemaphoreType.DMA((count,))],
        cost_estimate=pl.CostEstimate(flops=0, bytes_accessed=math.prod(shape), transcendentals=0),
        name="join",
    )(*parts)


def attend_kernel(place, kv, qx, above, below, far, taps, bias, res, conv, qs, xs, image):
    qs[0:EDGE] = above[2 * POS : 2 * POS + EDGE]
    qs[EDGE : EDGE + POS] = qx[0:POS]
    qs[EDGE + POS :] = below[2 * POS : 2 * POS + EDGE]
    xs[0:EDGE] = above[2 * POS + EDGE :]
    xs[EDGE : EDGE + POS] = qx[POS:]
    xs[EDGE + POS :] = below[2 * POS + EDGE :]
    tall = ROWS + 2 * MARGIN
    blank = jnp.zeros((tall, 8, HEAD_DIM), F32)
    image[:, 0:LEFT, :] = blank
    image[:, LEFT + IMG_W : LEFT + IMG_W + 8, :] = blank
    keys = [part[0:POS] for part in (kv, above, below, far)]
    values = [part[POS : 2 * POS] for part in (kv, above, below, far)]
    to_log2 = math.log2(math.e) / math.sqrt(HEAD_DIM)
    tile = 2 * IMG_W
    for t in range(tall // 2):
        own = slice(t * tile, (t + 1) * tile)
        queries = qs[own]
        scores = [
            lax.dot_general(queries, key, (((1,), (1,)), ((), ())), preferred_element_type=F32)
            for key in keys
        ]
        peak = functools.reduce(jnp.maximum, scores)
        peak = jnp.max(peak, axis=1, keepdims=True)
        weights = [jnp.exp2((score - peak) * to_log2) for score in scores]
        total = jnp.sum(functools.reduce(jnp.add, weights), axis=1, keepdims=True)
        summed = functools.reduce(
            jnp.add,
            [
                jnp.dot(weight.astype(BF16), value, preferred_element_type=F32)
                for weight, value in zip(weights, values)
            ],
        )
        out = (xs[own].astype(F32) + summed / total).astype(BF16).astype(F32)
        image[2 * t : 2 * t + 2, LEFT : LEFT + IMG_W, :] = out.reshape(2, IMG_W, HEAD_DIM)

    @pl.when(place[0] == 0)
    def _():
        image[0:MARGIN] = jnp.zeros((MARGIN, IMG_W + 16, HEAD_DIM), F32)

    @pl.when(place[0] == SEQ - 1)
    def _():
        image[tall - MARGIN :] = jnp.zeros((MARGIN, IMG_W + 16, HEAD_DIM), F32)

    for i in range(ROWS):
        res[i * IMG_W : (i + 1) * IMG_W] = image[MARGIN + i, LEFT : LEFT + IMG_W, :].astype(BF16)
    wide = 16
    for c0 in range(0, IMG_W, wide):
        sums = [jnp.broadcast_to(bias[...], (wide, HEAD_DIM)) for _ in range(ROWS)]
        for b in range(KERNEL):
            start = LEFT - MARGIN + b + c0
            columns = [image[r, start : start + wide, :] for r in range(tall)]
            for a in range(KERNEL):
                tap = taps[a * KERNEL + b : a * KERNEL + b + 1, :]
                for i in range(ROWS):
                    sums[i] = sums[i] + columns[i + a] * tap
        for i in range(ROWS):
            conv[i * IMG_W + c0 : i * IMG_W + c0 + wide] = sums[i].astype(BF16)


def attend(place, kv, qx, above, below, far, taps, bias):
    out = jax.ShapeDtypeStruct((POS, HEAD_DIM), BF16)
    vmem = pl.BlockSpec(memory_space=pltpu.VMEM)
    flops = 128 * (POS + 2 * EDGE) * SEQ * POS * HEAD_DIM
    return pl.pallas_call(
        attend_kernel,
        out_shape=(out, out),
        in_specs=[pl.BlockSpec(memory_space=pltpu.SMEM)] + [vmem] * 7,
        out_specs=(vmem, vmem),
        scratch_shapes=[
            pltpu.VMEM((POS + 2 * EDGE, HEAD_DIM), BF16),
            pltpu.VMEM((POS + 2 * EDGE, HEAD_DIM), BF16),
            pltpu.VMEM((ROWS + 2 * MARGIN, IMG_W + 16, HEAD_DIM), F32),
        ],
        compiler_params=pltpu.CompilerParams(vmem_limit_bytes=16 << 20),
        cost_estimate=pl.CostEstimate(flops=flops, bytes_accessed=2 << 20, transcendentals=2 << 20),
        name="attend",
    )(place, kv, qx, above, below, far, taps, bias)


AUX = 16


NEAR = (0, -1, 1, 2)
PIECES = 2 * len(NEAR)


def fetch(place, pieces, groups, slabs, sems):
    seq, row = place[1], place[2]
    rows = pieces[0].shape[1]
    copies = []
    for n, group in enumerate(groups):
        away = lax.rem(group // 2 - row // 2 + SEQ, SEQ)
        along_y = jnp.where(away == 3, 1, jnp.where(away == 0, 0, away + 1))
        same = lax.rem(group, 2) == lax.rem(row, 2)
        starts = [pl.multiple_of(lax.rem(seq + by + SEQ, SEQ) * rows, rows) for by in NEAR]
        mine, other = (
            [
                pltpu.make_async_copy(
                    piece.at[along_y], slabs.at[n, pl.ds(start, rows)], sems.at[n, i]
                )
                for i, (piece, start) in enumerate(zip(half, starts))
            ]
            for half in (pieces[: len(NEAR)], pieces[len(NEAR) :])
        )

        @pl.when(same)
        def _():
            for copy in mine:
                copy.start()

        @pl.when(jnp.logical_not(same))
        def _():
            for copy in other:
                copy.start()

        copies.append(mine)
    return copies


def slab_scratch(count, pieces):
    _, rows, columns = pieces[0].shape
    return [
        pltpu.VMEM((count, SEQ * rows, columns), BF16),
        pltpu.SemaphoreType.DMA((count, SEQ)),
    ]


def extra_rows(gain, offset, group):
    tiles = []
    for j in range(SEQ):
        here = pl.ds(j * CLASSES + group, 1)
        ratio = offset[here] / gain[here]
        high = ratio.astype(BF16).astype(F32)
        row = lax.broadcasted_iota(jnp.int32, (AUX, HEAD_DIM), 0)
        tile = jnp.where(row == 0, 1.0, 0.0)
        tile = jnp.where(row == 1, jnp.broadcast_to(high, tile.shape), tile)
        tile = jnp.where(row == 2, jnp.broadcast_to(ratio - high, tile.shape), tile)
        tiles.append(tile.astype(BF16))
    return jnp.concatenate(tiles, axis=1)


def product_of(blocks, copies, slab, gain, offset, group):
    left = jnp.concatenate([block[...] for block in blocks], axis=1)
    left = jnp.concatenate([left, extra_rows(gain, offset, group)], axis=0)
    for copy in copies:
        copy.wait()
    return jnp.dot(left, slab[...], preferred_element_type=F32)


def add_stats(blocks, pivot, before1, before2, sum1, sum2, rows=64):
    for t in range(0, POS, rows):
        here = slice(t, t + rows)
        centre, one, two = pivot[here], before1[here], before2[here]
        for block in blocks:
            away = block[here].astype(F32) - centre
            one = one + away
            two = two + away * away
        sum1[here] = one
        sum2[here] = two


def first_kernel(offsets, place, *refs):
    count = len(offsets)
    parts, refs = refs[:count], refs[count:]
    pieces, refs = refs[:PIECES], refs[PIECES:]
    gain, offset, acc, pivot, sum1, sum2, slabs, sems = refs
    groups = [lax.rem(place[0] + away + CLASSES, CLASSES) for away in offsets]
    copies = fetch(place, pieces, groups, slabs, sems)
    lead = jnp.mean(parts[0][0].astype(F32), axis=1, keepdims=True)
    pivot[...] = jnp.broadcast_to(lead, (POS, HEAD_DIM))
    sum1[...] = jnp.zeros((POS, HEAD_DIM), F32)
    sum2[...] = jnp.zeros((POS, HEAD_DIM), F32)
    for n, part in enumerate(parts):
        blocks = [part.at[j] for j in range(SEQ)]
        product = product_of(blocks, copies[n], slabs.at[n], gain, offset, groups[n])
        if n == 0:
            acc[...] = product
        else:
            acc[...] += product
        add_stats(blocks, pivot, sum1, sum2, sum1, sum2)


def more_kernel(offsets, place, *refs):
    count = len(offsets)
    parts, refs = refs[:count], refs[count:]
    acc, pivot, sum1, sum2, *refs = refs
    pieces, refs = refs[:PIECES], refs[PIECES:]
    gain, offset, acc_out, sum1_out, sum2_out, slabs, sems = refs
    groups = [lax.rem(place[0] + away + CLASSES, CLASSES) for away in offsets]
    copies = fetch(place, pieces, groups, slabs, sems)
    for n, part in enumerate(parts):
        blocks = [part.at[j] for j in range(SEQ)]
        before = (acc, sum1, sum2) if n == 0 else (acc_out, sum1_out, sum2_out)
        product = product_of(blocks, copies[n], slabs.at[n], gain, offset, groups[n])
        acc_out[...] = before[0][...] + product
        add_stats(blocks, pivot, before[1], before[2], sum1_out, sum2_out)


def stage(kernel, offsets, place, parts, before, pieces, gain, offset):
    vmem, here = pl.BlockSpec(memory_space=pltpu.VMEM), pl.BlockSpec(memory_space=pltpu.HBM)
    hidden = pieces[0].shape[-1]
    stat = jax.ShapeDtypeStruct((POS, HEAD_DIM), F32)
    total = jax.ShapeDtypeStruct((POS + AUX, hidden), F32)
    out_shape = (total, stat, stat) if before else (total, stat, stat, stat)
    return pl.pallas_call(
        functools.partial(kernel, offsets),
        out_shape=out_shape,
        in_specs=[pl.BlockSpec(memory_space=pltpu.SMEM)]
        + [vmem] * (len(parts) + len(before))
        + [here] * PIECES + [vmem, vmem],
        out_specs=(vmem,) * len(out_shape),
        scratch_shapes=slab_scratch(len(parts), pieces),
        compiler_params=pltpu.CompilerParams(vmem_limit_bytes=16 << 20),
        cost_estimate=pl.CostEstimate(
            flops=len(parts) << 28, bytes_accessed=len(parts) << 20, transcendentals=0
        ),
        name="stage",
    )(place, *parts, *before, *pieces, gain, offset)


def last_kernel(place, *refs):
    acc, pivot, sum1, sum2, above, below, *refs = refs
    pieces, refs = refs[:PIECES], refs[PIECES:]
    gain, offset, bias, out, one, two, slabs, sems = refs
    group = lax.rem(place[0] + 4, CLASSES)
    (copies,) = fetch(place, pieces, [group], slabs, sems)
    blocks = [above.at[0], above.at[1], below.at[0], below.at[1]]
    add_stats(blocks, pivot, sum1, sum2, one, two)
    product = acc[...] + product_of(blocks, copies, slabs.at[0], gain, offset, group)
    mean1 = jnp.sum(one[...], axis=1, keepdims=True) * (1.0 / C)
    mean2 = jnp.sum(two[...], axis=1, keepdims=True) * (1.0 / C)
    centre = pivot[:, 0:1] + mean1
    spread = jnp.maximum(mean2 - mean1 * mean1, 0.0)
    scale = lax.rsqrt(spread + 1e-06)
    slope = product[POS : POS + 1]
    level = product[POS + 1 : POS + 2] + product[POS + 2 : POS + 3] + bias[...]
    project = scale * (product[0:POS] - centre * slope) + level
    out[...] = (0.5 * project * (1.0 + lax.erf(project * math.sqrt(0.5)))).astype(BF16)


def last(place, acc, stats, above, below, pieces, gain, offset, bias):
    vmem, here = pl.BlockSpec(memory_space=pltpu.VMEM), pl.BlockSpec(memory_space=pltpu.HBM)
    hidden = pieces[0].shape[-1]
    return pl.pallas_call(
        last_kernel,
        out_shape=jax.ShapeDtypeStruct((POS, hidden), BF16),
        in_specs=[pl.BlockSpec(memory_space=pltpu.SMEM)] + [vmem] * 6 + [here] * PIECES + [vmem] * 3,
        out_specs=vmem,
        scratch_shapes=[pltpu.VMEM((POS, HEAD_DIM), F32)] * 2 + slab_scratch(1, pieces),
        compiler_params=pltpu.CompilerParams(vmem_limit_bytes=16 << 20),
        cost_estimate=pl.CostEstimate(flops=1 << 28, bytes_accessed=7 << 20, transcendentals=1 << 18),
        name="last",
    )(place, acc, *stats, above, below, *pieces, gain, offset, bias)


def on_device(
    inputs,
    query_proj,
    key_proj,
    value_proj,
    depth_weight,
    depth_bias,
    norm_gain,
    norm_bias,
    expand_weight,
    expand_bias,
):
    seq, row, col = (lax.axis_index(axis) for axis in ("seq", "row", "col"))
    depth, hidden = expand_weight.shape
    gain, offset = (a.reshape(C // depth, depth) for a in (norm_gain, norm_bias))
    x, q, k, v = (a.reshape(POS, HEAD_DIM) for a in (inputs, query_proj, key_proj, value_proj))
    x, q, k, v = (pltpu.with_memory_space_constraint(a, pltpu.HBM) for a in (x, q, k, v))
    mine = (seq * CLASSES + row).astype(jnp.int32).reshape(1)
    held = (pltpu.with_memory_space_constraint(a, pltpu.HBM) for a in (expand_weight, gain))
    kv, upper, scaled = scale(mine, k, v, q, x, *held)
    far, below = shift(kv, "seq", 2), shift(upper, "seq", -1)
    qx, lower = pack(k, v, q, x)
    above = shift(lower, "seq", 1)
    along_y = join([scaled] + [shift(scaled, "row", 2 * by) for by in (1, -1, 2)])
    far, above, below, along_y = lax.optimization_barrier((far, above, below, along_y))
    along_x = [along_y] + [shift(along_y, "seq", by) for by in (1, -1, 2)]
    gain, offset = gain.astype(F32), offset.astype(F32)
    taps = depth_weight.astype(F32).reshape(KERNEL * KERNEL, HEAD_DIM)
    bias = depth_bias.astype(F32).reshape(1, HEAD_DIM)
    residual, convolved = attend(
        seq.astype(jnp.int32).reshape(1), kv, qx, above, below, far, taps, bias
    )

    strides = [[i + CLASSES * j for j in range(SEQ)] for i in range(CLASSES)]
    own = lax.all_gather(convolved, "col", axis=0, tiled=True, axis_index_groups=strides)
    own = own.reshape(SEQ, POS, HEAD_DIM)
    own, *along_x = lax.optimization_barrier((own, *along_x))
    swap = [(i, i ^ 1) for i in range(lax.axis_size("row"))]
    pairs, up, down, pieces = [], own, own, []
    for n in range(3):
        up, down = shift(up, "col", 1), shift(down, "col", -1)
        two = [lax.ppermute(piece, "row", swap) for piece in along_x[2 * n - 2 : 2 * n]] if n else []
        up, down, *two = lax.optimization_barrier((up, down, *two))
        pairs.append((up, down))
        pieces += two
    pieces = [pltpu.with_memory_space_constraint(a, pltpu.HBM) for a in along_x + pieces]
    place = jnp.stack([col, seq, row]).astype(jnp.int32)
    parts = (own, *pairs[0], *pairs[1])
    before = stage(first_kernel, (0, -1, 1, -2, 2), place, parts, (), pieces, gain, offset)
    up, down = shift(up[:2], "col", 1), shift(down[2:], "col", -1)
    acc, *sums = stage(more_kernel, (-3, 3), place, pairs[2], before, pieces, gain, offset)
    pivot = before[1]
    bias = expand_bias.astype(F32).reshape(1, hidden)
    out = last(place, acc, (pivot, *sums), up, down, pieces, gain, offset, bias)
    return (
        residual.reshape(inputs.shape),
        out.reshape(inputs.shape[:3] + (hidden,)),
    )


def solution(mesh):
    return jax.shard_map(
        on_device,
        mesh=mesh,
        in_specs=(
            P("row", "seq", None, "col"),
            P("row", "seq", None, "col"),
            P("row", "seq", None, "col"),
            P("row", "seq", None, "col"),
            P(None, None, "col"),
            P("col"),
            P(),
            P(),
            P(("seq", "row"), "col"),
            P("col"),
        ),
        out_specs=(P("row", "seq", None, "col"), P("row", "seq", None, "col")),
        check_vma=False,
    )
```

```python
import functools
import math

import jax
import jax.numpy as jnp
from jax import lax
from jax.experimental import pallas as pl
from jax.experimental.pallas import tpu as pltpu
from jax.sharding import PartitionSpec as P

HEAD_DIM = 128
KERNEL = 7
MARGIN = KERNEL // 2
IMG_W = 64
ROWS = 8
POS = ROWS * IMG_W
EDGE = MARGIN * IMG_W
C = 4096
SEQ = 4
CLASSES = 8
LEFT = 8
F32 = jnp.float32
BF16 = jnp.bfloat16


def shift(array, axis, by):
    peers = lax.axis_size(axis)
    return lax.ppermute(array, axis, [(i, (i + by) % peers) for i in range(peers)])


def move(pairs, sems):
    copies = [pltpu.make_async_copy(a, b, sems.at[i]) for i, (a, b) in enumerate(pairs)]
    for copy in copies:
        copy.start()
    return copies


def message_moves(k, v, q, x, message, edge):
    return [
        (k, message.at[0:POS]),
        (v, message.at[POS : 2 * POS]),
        (q.at[edge], message.at[2 * POS : 2 * POS + EDGE]),
        (x.at[edge], message.at[2 * POS + EDGE :]),
    ]


def pack_kernel(k, v, q, x, qx, lower, sems):
    own = [(q, qx.at[0:POS]), (x, qx.at[POS:])]
    edge = slice(POS - EDGE, POS)
    for copy in move(own + message_moves(k, v, q, x, lower, edge), sems):
        copy.wait()


def pack(k, v, q, x):
    vmem, here = pl.BlockSpec(memory_space=pltpu.VMEM), pl.BlockSpec(memory_space=pltpu.HBM)
    two = jax.ShapeDtypeStruct((2 * POS, HEAD_DIM), BF16)
    message = jax.ShapeDtypeStruct((2 * (POS + EDGE), HEAD_DIM), BF16)
    return pl.pallas_call(
        pack_kernel,
        out_shape=(two, message),
        in_specs=[here] * 4,
        out_specs=(vmem,) * 2,
        scratch_shapes=[pltpu.SemaphoreType.DMA((6,))],
        compiler_params=pltpu.CompilerParams(vmem_limit_bytes=8 << 20),
        name="pack",
    )(k, v, q, x)


def scale_kernel(place, k, v, q, x, weight_in, gain_in, kv, upper, scaled, weight, gain, sems):
    pairs = [(weight_in, weight), (gain_in, gain), (k, kv.at[0:POS]), (v, kv.at[POS:])]
    copies = move(pairs + message_moves(k, v, q, x, upper, slice(0, EDGE)), sems)
    for copy in copies[:2]:
        copy.wait()
    depth = weight.shape[0]
    gains = gain[...].astype(F32)
    line = lax.broadcasted_iota(jnp.int32, gains.shape, 0) == place[0]
    mine = jnp.sum(jnp.where(line, gains, 0.0), axis=0, keepdims=True)
    mine = jnp.transpose(jnp.broadcast_to(mine, (depth, depth)))
    for c in range(0, weight.shape[1], depth):
        scaled[:, c : c + depth] = (weight[:, c : c + depth].astype(F32) * mine).astype(BF16)
    for copy in copies[2:]:
        copy.wait()


def scale(place, k, v, q, x, weight, gain):
    vmem, here = pl.BlockSpec(memory_space=pltpu.VMEM), pl.BlockSpec(memory_space=pltpu.HBM)
    message = jax.ShapeDtypeStruct((2 * (POS + EDGE), HEAD_DIM), BF16)
    return pl.pallas_call(
        scale_kernel,
        out_shape=(
            jax.ShapeDtypeStruct((2 * POS, HEAD_DIM), BF16),
            message,
            jax.ShapeDtypeStruct(weight.shape, BF16),
        ),
        in_specs=[pl.BlockSpec(memory_space=pltpu.SMEM)] + [here] * 6,
        out_specs=(vmem,) * 3,
        scratch_shapes=[
            pltpu.VMEM(weight.shape, BF16),
            pltpu.VMEM(gain.shape, BF16),
            pltpu.SemaphoreType.DMA((8,)),
        ],
        compiler_params=pltpu.CompilerParams(vmem_limit_bytes=8 << 20),
        name="scale",
    )(place, k, v, q, x, weight, gain)


TALL = ROWS + 2 * MARGIN
TO_LOG2 = math.log2(math.e) / math.sqrt(HEAD_DIM)
TILE = 2 * IMG_W


def spread_rows(above, own, below, rows, at):
    rows[0:EDGE] = above[at : at + EDGE]
    rows[EDGE : EDGE + POS] = own
    rows[EDGE + POS :] = below[at : at + EDGE]


def weigh(queries, parts, peak):
    scores = [
        lax.dot_general(queries, part[0:POS], (((1,), (1,)), ((), ())), preferred_element_type=F32)
        for part in parts
    ]
    highest = jnp.max(functools.reduce(jnp.maximum, scores), axis=1, keepdims=True)
    if peak is not None:
        highest = jnp.maximum(highest, peak)
    weights = [jnp.exp2((score - highest) * TO_LOG2) for score in scores]
    total = jnp.sum(functools.reduce(jnp.add, weights), axis=1, keepdims=True)
    summed = functools.reduce(
        jnp.add,
        [
            jnp.dot(weight.astype(BF16), part[POS : 2 * POS], preferred_element_type=F32)
            for weight, part in zip(weights, parts)
        ],
    )
    return highest, total, summed


def near_kernel(kv, qx, above, below, summed_out, peak_out, total_out, qs):
    spread_rows(above, qx[0:POS], below, qs, 2 * POS)
    for t in range(TALL // 2):
        own = slice(t * TILE, (t + 1) * TILE)
        peak, total, summed = weigh(qs[own], (kv, above, below), None)
        summed_out[own] = summed
        peak_out[own] = jnp.broadcast_to(peak, summed.shape)
        total_out[own] = jnp.broadcast_to(total, summed.shape)


def near(kv, qx, above, below):
    vmem = pl.BlockSpec(memory_space=pltpu.VMEM)
    out = jax.ShapeDtypeStruct((POS + 2 * EDGE, HEAD_DIM), F32)
    flops = 3 * (POS + 2 * EDGE) * SEQ * POS * HEAD_DIM
    return pl.pallas_call(
        near_kernel,
        out_shape=(out,) * 3,
        in_specs=[vmem] * 4,
        out_specs=(vmem,) * 3,
        scratch_shapes=[pltpu.VMEM((POS + 2 * EDGE, HEAD_DIM), BF16)],
        compiler_params=pltpu.CompilerParams(vmem_limit_bytes=16 << 20),
        cost_estimate=pl.CostEstimate(flops=flops, bytes_accessed=3 << 20, transcendentals=2 << 20),
        name="near",
    )(kv, qx, above, below)


def attend_kernel(place, qx, above, below, far, summed_in, peak_in, total_in, taps, bias, res, conv, qs, xs, image):
    spread_rows(above, qx[0:POS], below, qs, 2 * POS)
    spread_rows(above, qx[POS:], below, xs, 2 * POS + EDGE)
    tall = TALL
    blank = jnp.zeros((tall, 8, HEAD_DIM), F32)
    image[:, 0:LEFT, :] = blank
    image[:, LEFT + IMG_W : LEFT + IMG_W + 8, :] = blank
    for t in range(tall // 2):
        own = slice(t * TILE, (t + 1) * TILE)
        before = peak_in[own]
        peak, total, summed = weigh(qs[own], (far,), before[:, 0:1])
        factor = jnp.exp2((before - peak) * TO_LOG2)
        total = total_in[own] * factor + total
        summed = summed_in[own] * factor + summed
        out = (xs[own].astype(F32) + summed / total).astype(BF16).astype(F32)
        image[2 * t : 2 * t + 2, LEFT : LEFT + IMG_W, :] = out.reshape(2, IMG_W, HEAD_DIM)

    @pl.when(place[0] == 0)
    def _():
        image[0:MARGIN] = jnp.zeros((MARGIN, IMG_W + 16, HEAD_DIM), F32)

    @pl.when(place[0] == SEQ - 1)
    def _():
        image[tall - MARGIN :] = jnp.zeros((MARGIN, IMG_W + 16, HEAD_DIM), F32)

    for i in range(ROWS):
        res[i * IMG_W : (i + 1) * IMG_W] = image[MARGIN + i, LEFT : LEFT + IMG_W, :].astype(BF16)
    wide = 16
    for c0 in range(0, IMG_W, wide):
        sums = [jnp.broadcast_to(bias[...], (wide, HEAD_DIM)) for _ in range(ROWS)]
        for b in range(KERNEL):
            start = LEFT - MARGIN + b + c0
            columns = [image[r, start : start + wide, :] for r in range(tall)]
            for a in range(KERNEL):
                tap = taps[a * KERNEL + b : a * KERNEL + b + 1, :]
                for i in range(ROWS):
                    sums[i] = sums[i] + columns[i + a] * tap
        for i in range(ROWS):
            conv[i * IMG_W + c0 : i * IMG_W + c0 + wide] = sums[i].astype(BF16)


def attend(place, qx, above, below, far, begun, taps, bias):
    out = jax.ShapeDtypeStruct((POS, HEAD_DIM), BF16)
    vmem = pl.BlockSpec(memory_space=pltpu.VMEM)
    flops = (POS + 2 * EDGE) * SEQ * POS * HEAD_DIM
    return pl.pallas_call(
        attend_kernel,
        out_shape=(out, out),
        in_specs=[pl.BlockSpec(memory_space=pltpu.SMEM)] + [vmem] * 9,
        out_specs=(vmem, vmem),
        scratch_shapes=[
            pltpu.VMEM((POS + 2 * EDGE, HEAD_DIM), BF16),
            pltpu.VMEM((POS + 2 * EDGE, HEAD_DIM), BF16),
            pltpu.VMEM((TALL, IMG_W + 16, HEAD_DIM), F32),
        ],
        compiler_params=pltpu.CompilerParams(vmem_limit_bytes=16 << 20),
        cost_estimate=pl.CostEstimate(flops=flops, bytes_accessed=2 << 20, transcendentals=1 << 19),
        name="attend",
    )(place, qx, above, below, far, *begun, taps, bias)


AUX = 16


def fetch(weights, groups, slabs, sems):
    copies = []
    for n, group in enumerate(groups):
        rows = weights.shape[2]
        copies.append(
            [
                pltpu.make_async_copy(
                    weights.at[j, group], slabs.at[n, j * rows : (j + 1) * rows], sems.at[n, j]
                )
                for j in range(SEQ)
            ]
        )
        for copy in copies[-1]:
            copy.start()
    return copies


def slab_scratch(count, weights):
    _, _, rows, columns = weights.shape
    return [
        pltpu.VMEM((count, SEQ * rows, columns), BF16),
        pltpu.SemaphoreType.DMA((count, SEQ)),
    ]


def extra_rows(gain, offset, group):
    tiles = []
    for j in range(SEQ):
        here = pl.ds(j * CLASSES + group, 1)
        ratio = offset[here] / gain[here]
        high = ratio.astype(BF16).astype(F32)
        row = lax.broadcasted_iota(jnp.int32, (AUX, HEAD_DIM), 0)
        tile = jnp.where(row == 0, 1.0, 0.0)
        tile = jnp.where(row == 1, jnp.broadcast_to(high, tile.shape), tile)
        tile = jnp.where(row == 2, jnp.broadcast_to(ratio - high, tile.shape), tile)
        tiles.append(tile.astype(BF16))
    return jnp.concatenate(tiles, axis=1)


def product_of(blocks, copies, slab, gain, offset, group):
    left = jnp.concatenate([block[...] for block in blocks], axis=1)
    left = jnp.concatenate([left, extra_rows(gain, offset, group)], axis=0)
    for copy in copies:
        copy.wait()
    return jnp.dot(left, slab[...], preferred_element_type=F32)


def add_stats(blocks, pivot, before1, before2, sum1, sum2, rows=64):
    for t in range(0, POS, rows):
        here = slice(t, t + rows)
        centre, one, two = pivot[here], before1[here], before2[here]
        for block in blocks:
            away = block[here].astype(F32) - centre
            one = one + away
            two = two + away * away
        sum1[here] = one
        sum2[here] = two


def first_kernel(offsets, place, *refs):
    count = len(offsets)
    parts, refs = refs[:count], refs[count:]
    weights, gain, offset, acc, pivot, sum1, sum2, slabs, sems = refs
    groups = [lax.rem(place[0] + away + CLASSES, CLASSES) for away in offsets]
    copies = fetch(weights, groups, slabs, sems)
    lead = jnp.mean(parts[0][0].astype(F32), axis=1, keepdims=True)
    pivot[...] = jnp.broadcast_to(lead, (POS, HEAD_DIM))
    sum1[...] = jnp.zeros((POS, HEAD_DIM), F32)
    sum2[...] = jnp.zeros((POS, HEAD_DIM), F32)
    for n, part in enumerate(parts):
        blocks = [part.at[j] for j in range(SEQ)]
        product = product_of(blocks, copies[n], slabs.at[n], gain, offset, groups[n])
        if n == 0:
            acc[...] = product
        else:
            acc[...] += product
        add_stats(blocks, pivot, sum1, sum2, sum1, sum2)


def more_kernel(offsets, place, *refs):
    count = len(offsets)
    parts, refs = refs[:count], refs[count:]
    acc, pivot, sum1, sum2, weights, gain, offset, acc_out, sum1_out, sum2_out, slabs, sems = refs
    groups = [lax.rem(place[0] + away + CLASSES, CLASSES) for away in offsets]
    copies = fetch(weights, groups, slabs, sems)
    for n, part in enumerate(parts):
        blocks = [part.at[j] for j in range(SEQ)]
        before = (acc, sum1, sum2) if n == 0 else (acc_out, sum1_out, sum2_out)
        product = product_of(blocks, copies[n], slabs.at[n], gain, offset, groups[n])
        acc_out[...] = before[0][...] + product
        add_stats(blocks, pivot, before[1], before[2], sum1_out, sum2_out)


def stage(kernel, offsets, place, parts, before, weights, gain, offset):
    vmem, here = pl.BlockSpec(memory_space=pltpu.VMEM), pl.BlockSpec(memory_space=pltpu.HBM)
    hidden = weights.shape[-1]
    stat = jax.ShapeDtypeStruct((POS, HEAD_DIM), F32)
    total = jax.ShapeDtypeStruct((POS + AUX, hidden), F32)
    out_shape = (total, stat, stat) if before else (total, stat, stat, stat)
    return pl.pallas_call(
        functools.partial(kernel, offsets),
        out_shape=out_shape,
        in_specs=[pl.BlockSpec(memory_space=pltpu.SMEM)]
        + [vmem] * (len(parts) + len(before))
        + [here, vmem, vmem],
        out_specs=(vmem,) * len(out_shape),
        scratch_shapes=slab_scratch(len(parts), weights),
        compiler_params=pltpu.CompilerParams(vmem_limit_bytes=16 << 20),
        cost_estimate=pl.CostEstimate(
            flops=len(parts) << 28, bytes_accessed=len(parts) << 20, transcendentals=0
        ),
        name="stage",
    )(place, *parts, *before, weights, gain, offset)


def last_kernel(place, *refs):
    acc, pivot, sum1, sum2, above, below, weights, gain, offset, bias, out, one, two, slabs, sems = refs
    group = lax.rem(place[0] + 4, CLASSES)
    (copies,) = fetch(weights, [group], slabs, sems)
    blocks = [above.at[0], above.at[1], below.at[0], below.at[1]]
    add_stats(blocks, pivot, sum1, sum2, one, two)
    product = acc[...] + product_of(blocks, copies, slabs.at[0], gain, offset, group)
    mean1 = jnp.sum(one[...], axis=1, keepdims=True) * (1.0 / C)
    mean2 = jnp.sum(two[...], axis=1, keepdims=True) * (1.0 / C)
    centre = pivot[:, 0:1] + mean1
    spread = jnp.maximum(mean2 - mean1 * mean1, 0.0)
    scale = lax.rsqrt(spread + 1e-06)
    slope = product[POS : POS + 1]
    level = product[POS + 1 : POS + 2] + product[POS + 2 : POS + 3] + bias[...]
    project = scale * (product[0:POS] - centre * slope) + level
    out[...] = (0.5 * project * (1.0 + lax.erf(project * math.sqrt(0.5)))).astype(BF16)


def last(place, acc, stats, above, below, weights, gain, offset, bias):
    vmem, here = pl.BlockSpec(memory_space=pltpu.VMEM), pl.BlockSpec(memory_space=pltpu.HBM)
    hidden = weights.shape[-1]
    return pl.pallas_call(
        last_kernel,
        out_shape=jax.ShapeDtypeStruct((POS, hidden), BF16),
        in_specs=[pl.BlockSpec(memory_space=pltpu.SMEM)] + [vmem] * 6 + [here] + [vmem] * 3,
        out_specs=vmem,
        scratch_shapes=[pltpu.VMEM((POS, HEAD_DIM), F32)] * 2 + slab_scratch(1, weights),
        compiler_params=pltpu.CompilerParams(vmem_limit_bytes=16 << 20),
        cost_estimate=pl.CostEstimate(flops=1 << 28, bytes_accessed=7 << 20, transcendentals=1 << 18),
        name="last",
    )(place, acc, *stats, above, below, weights, gain, offset, bias)


def on_device(
    inputs,
    query_proj,
    key_proj,
    value_proj,
    depth_weight,
    depth_bias,
    norm_gain,
    norm_bias,
    expand_weight,
    expand_bias,
):
    seq, row, col = (lax.axis_index(axis) for axis in ("seq", "row", "col"))
    depth, hidden = expand_weight.shape
    gain, offset = (a.reshape(C // depth, depth) for a in (norm_gain, norm_bias))
    x, q, k, v = (a.reshape(POS, HEAD_DIM) for a in (inputs, query_proj, key_proj, value_proj))
    x, q, k, v = (pltpu.with_memory_space_constraint(a, pltpu.HBM) for a in (x, q, k, v))
    mine = (seq * CLASSES + row).astype(jnp.int32).reshape(1)
    held = (pltpu.with_memory_space_constraint(a, pltpu.HBM) for a in (expand_weight, gain))
    qx, lower = pack(k, v, q, x)
    above = shift(lower, "seq", 1)
    kv, upper, scaled = scale(mine, k, v, q, x, *held)
    below, far = shift(upper, "seq", -1), shift(kv, "seq", 2)
    weights = lax.all_gather(scaled, ("seq", "row"), axis=0, tiled=True)
    weights = weights.reshape(SEQ, CLASSES, depth, hidden)
    weights = pltpu.with_memory_space_constraint(weights, pltpu.HBM)
    gain, offset = gain.astype(F32), offset.astype(F32)
    taps = depth_weight.astype(F32).reshape(KERNEL * KERNEL, HEAD_DIM)
    bias = depth_bias.astype(F32).reshape(1, HEAD_DIM)
    begun = near(kv, qx, above, below)
    residual, convolved = attend(
        seq.astype(jnp.int32).reshape(1), qx, above, below, far, begun, taps, bias
    )

    strides = [[i + CLASSES * j for j in range(SEQ)] for i in range(CLASSES)]
    own = lax.all_gather(convolved, "col", axis=0, tiled=True, axis_index_groups=strides)
    own = own.reshape(SEQ, POS, HEAD_DIM)
    pairs, up, down = [], own, own
    for _ in range(3):
        up, down = shift(up, "col", 1), shift(down, "col", -1)
        pairs.append((up, down))
    place = col.astype(jnp.int32).reshape(1)
    parts = (own, *pairs[0], *pairs[1])
    before = stage(first_kernel, (0, -1, 1, -2, 2), place, parts, (), weights, gain, offset)
    up, down, before = lax.optimization_barrier((up, down, before))
    pairs[2] = (up, down)
    up, down = shift(up[:2], "col", 1), shift(down[2:], "col", -1)
    acc, *sums = stage(more_kernel, (-3, 3), place, pairs[2], before, weights, gain, offset)
    pivot = before[1]
    bias = expand_bias.astype(F32).reshape(1, hidden)
    out = last(place, acc, (pivot, *sums), up, down, weights, gain, offset, bias)
    return (
        residual.reshape(inputs.shape),
        out.reshape(inputs.shape[:3] + (hidden,)),
    )


def solution(mesh):
    return jax.shard_map(
        on_device,
        mesh=mesh,
        in_specs=(
            P("row", "seq", None, "col"),
            P("row", "seq", None, "col"),
            P("row", "seq", None, "col"),
            P("row", "seq", None, "col"),
            P(None, None, "col"),
            P("col"),
            P(),
            P(),
            P(("seq", "row"), "col"),
            P("col"),
        ),
        out_specs=(P("row", "seq", None, "col"), P("row", "seq", None, "col")),
        check_vma=False,
    )
```

```python
import functools
import math

import jax
import jax.numpy as jnp
from jax import lax
from jax.experimental import pallas as pl
from jax.experimental.pallas import tpu as pltpu
from jax.sharding import PartitionSpec as P

HEAD_DIM = 128
KERNEL = 7
MARGIN = KERNEL // 2
IMG_W = 64
ROWS = 8
POS = ROWS * IMG_W
EDGE = MARGIN * IMG_W
C = 4096
SEQ = 4
CLASSES = 8
LEFT = 8
F32 = jnp.float32
BF16 = jnp.bfloat16


def shift(array, axis, by):
    peers = lax.axis_size(axis)
    return lax.ppermute(array, axis, [(i, (i + by) % peers) for i in range(peers)])


def move(pairs, sems):
    copies = [pltpu.make_async_copy(a, b, sems.at[i]) for i, (a, b) in enumerate(pairs)]
    for copy in copies:
        copy.start()
    return copies


def message_moves(k, v, q, x, message, edge):
    return [
        (k, message.at[0:POS]),
        (v, message.at[POS : 2 * POS]),
        (q.at[edge], message.at[2 * POS : 2 * POS + EDGE]),
        (x.at[edge], message.at[2 * POS + EDGE :]),
    ]


def pack_kernel(k, v, q, x, qx, lower, sems):
    own = [(q, qx.at[0:POS]), (x, qx.at[POS:])]
    edge = slice(POS - EDGE, POS)
    for copy in move(own + message_moves(k, v, q, x, lower, edge), sems):
        copy.wait()


def pack(k, v, q, x):
    vmem, here = pl.BlockSpec(memory_space=pltpu.VMEM), pl.BlockSpec(memory_space=pltpu.HBM)
    two = jax.ShapeDtypeStruct((2 * POS, HEAD_DIM), BF16)
    message = jax.ShapeDtypeStruct((2 * (POS + EDGE), HEAD_DIM), BF16)
    return pl.pallas_call(
        pack_kernel,
        out_shape=(two, message),
        in_specs=[here] * 4,
        out_specs=(vmem,) * 2,
        scratch_shapes=[pltpu.SemaphoreType.DMA((6,))],
        compiler_params=pltpu.CompilerParams(vmem_limit_bytes=8 << 20),
        name="pack",
    )(k, v, q, x)


def scale_kernel(place, k, v, q, x, weight_in, gain_in, kv, upper, scaled, weight, gain, sems):
    pairs = [(weight_in, weight), (gain_in, gain), (k, kv.at[0:POS]), (v, kv.at[POS:])]
    copies = move(pairs + message_moves(k, v, q, x, upper, slice(0, EDGE)), sems)
    for copy in copies[:2]:
        copy.wait()
    depth = weight.shape[0]
    gains = gain[...].astype(F32)
    line = lax.broadcasted_iota(jnp.int32, gains.shape, 0) == place[0]
    mine = jnp.sum(jnp.where(line, gains, 0.0), axis=0, keepdims=True)
    mine = jnp.transpose(jnp.broadcast_to(mine, (depth, depth)))
    for c in range(0, weight.shape[1], depth):
        scaled[:, c : c + depth] = (weight[:, c : c + depth].astype(F32) * mine).astype(BF16)
    for copy in copies[2:]:
        copy.wait()


def scale(place, k, v, q, x, weight, gain):
    vmem, here = pl.BlockSpec(memory_space=pltpu.VMEM), pl.BlockSpec(memory_space=pltpu.HBM)
    message = jax.ShapeDtypeStruct((2 * (POS + EDGE), HEAD_DIM), BF16)
    return pl.pallas_call(
        scale_kernel,
        out_shape=(
            jax.ShapeDtypeStruct((2 * POS, HEAD_DIM), BF16),
            message,
            jax.ShapeDtypeStruct(weight.shape, BF16),
        ),
        in_specs=[pl.BlockSpec(memory_space=pltpu.SMEM)] + [here] * 6,
        out_specs=(vmem,) * 3,
        scratch_shapes=[
            pltpu.VMEM(weight.shape, BF16),
            pltpu.VMEM(gain.shape, BF16),
            pltpu.SemaphoreType.DMA((8,)),
        ],
        compiler_params=pltpu.CompilerParams(vmem_limit_bytes=8 << 20),
        name="scale",
    )(place, k, v, q, x, weight, gain)


TALL = ROWS + 2 * MARGIN
TO_LOG2 = math.log2(math.e) / math.sqrt(HEAD_DIM)
TILE = 2 * IMG_W


def spread_rows(above, own, below, rows, at):
    rows[0:EDGE] = above[at : at + EDGE]
    rows[EDGE : EDGE + POS] = own
    rows[EDGE + POS :] = below[at : at + EDGE]


def weigh(queries, parts, peak):
    scores = [
        lax.dot_general(queries, part[0:POS], (((1,), (1,)), ((), ())), preferred_element_type=F32)
        for part in parts
    ]
    highest = jnp.max(functools.reduce(jnp.maximum, scores), axis=1, keepdims=True)
    if peak is not None:
        highest = jnp.maximum(highest, peak)
    weights = [jnp.exp2((score - highest) * TO_LOG2) for score in scores]
    total = jnp.sum(functools.reduce(jnp.add, weights), axis=1, keepdims=True)
    summed = functools.reduce(
        jnp.add,
        [
            jnp.dot(weight.astype(BF16), part[POS : 2 * POS], preferred_element_type=F32)
            for weight, part in zip(weights, parts)
        ],
    )
    return highest, total, summed


def near_kernel(kv, qx, above, below, summed_out, peak_out, total_out, qs):
    spread_rows(above, qx[0:POS], below, qs, 2 * POS)
    for t in range(TALL // 2):
        own = slice(t * TILE, (t + 1) * TILE)
        peak, total, summed = weigh(qs[own], (kv, above, below), None)
        summed_out[own] = summed
        peak_out[own] = jnp.broadcast_to(peak, summed.shape)
        total_out[own] = jnp.broadcast_to(total, summed.shape)


def near(kv, qx, above, below):
    vmem = pl.BlockSpec(memory_space=pltpu.VMEM)
    out = jax.ShapeDtypeStruct((POS + 2 * EDGE, HEAD_DIM), F32)
    flops = 3 * (POS + 2 * EDGE) * SEQ * POS * HEAD_DIM
    return pl.pallas_call(
        near_kernel,
        out_shape=(out,) * 3,
        in_specs=[vmem] * 4,
        out_specs=(vmem,) * 3,
        scratch_shapes=[pltpu.VMEM((POS + 2 * EDGE, HEAD_DIM), BF16)],
        compiler_params=pltpu.CompilerParams(vmem_limit_bytes=16 << 20),
        cost_estimate=pl.CostEstimate(flops=flops, bytes_accessed=3 << 20, transcendentals=2 << 20),
        name="near",
    )(kv, qx, above, below)


def attend_kernel(place, qx, above, below, far, summed_in, peak_in, total_in, taps, bias, res, conv, qs, xs, image):
    spread_rows(above, qx[0:POS], below, qs, 2 * POS)
    spread_rows(above, qx[POS:], below, xs, 2 * POS + EDGE)
    tall = TALL
    blank = jnp.zeros((tall, 8, HEAD_DIM), F32)
    image[:, 0:LEFT, :] = blank
    image[:, LEFT + IMG_W : LEFT + IMG_W + 8, :] = blank
    for t in range(tall // 2):
        own = slice(t * TILE, (t + 1) * TILE)
        before = peak_in[own]
        peak, total, summed = weigh(qs[own], (far,), before[:, 0:1])
        factor = jnp.exp2((before - peak) * TO_LOG2)
        total = total_in[own] * factor + total
        summed = summed_in[own] * factor + summed
        out = (xs[own].astype(F32) + summed / total).astype(BF16).astype(F32)
        image[2 * t : 2 * t + 2, LEFT : LEFT + IMG_W, :] = out.reshape(2, IMG_W, HEAD_DIM)

    @pl.when(place[0] == 0)
    def _():
        image[0:MARGIN] = jnp.zeros((MARGIN, IMG_W + 16, HEAD_DIM), F32)

    @pl.when(place[0] == SEQ - 1)
    def _():
        image[tall - MARGIN :] = jnp.zeros((MARGIN, IMG_W + 16, HEAD_DIM), F32)

    for i in range(ROWS):
        res[i * IMG_W : (i + 1) * IMG_W] = image[MARGIN + i, LEFT : LEFT + IMG_W, :].astype(BF16)
    wide = 16
    for c0 in range(0, IMG_W, wide):
        sums = [jnp.broadcast_to(bias[...], (wide, HEAD_DIM)) for _ in range(ROWS)]
        for b in range(KERNEL):
            start = LEFT - MARGIN + b + c0
            columns = [image[r, start : start + wide, :] for r in range(tall)]
            for a in range(KERNEL):
                tap = taps[a * KERNEL + b : a * KERNEL + b + 1, :]
                for i in range(ROWS):
                    sums[i] = sums[i] + columns[i + a] * tap
        for i in range(ROWS):
            conv[i * IMG_W + c0 : i * IMG_W + c0 + wide] = sums[i].astype(BF16)


def attend(place, qx, above, below, far, begun, taps, bias):
    out = jax.ShapeDtypeStruct((POS, HEAD_DIM), BF16)
    vmem = pl.BlockSpec(memory_space=pltpu.VMEM)
    flops = (POS + 2 * EDGE) * SEQ * POS * HEAD_DIM
    return pl.pallas_call(
        attend_kernel,
        out_shape=(out, out),
        in_specs=[pl.BlockSpec(memory_space=pltpu.SMEM)] + [vmem] * 9,
        out_specs=(vmem, vmem),
        scratch_shapes=[
            pltpu.VMEM((POS + 2 * EDGE, HEAD_DIM), BF16),
            pltpu.VMEM((POS + 2 * EDGE, HEAD_DIM), BF16),
            pltpu.VMEM((TALL, IMG_W + 16, HEAD_DIM), F32),
        ],
        compiler_params=pltpu.CompilerParams(vmem_limit_bytes=16 << 20),
        cost_estimate=pl.CostEstimate(flops=flops, bytes_accessed=2 << 20, transcendentals=1 << 19),
        name="attend",
    )(place, qx, above, below, far, *begun, taps, bias)


AUX = 16


def fetch(weights, groups, slabs, sems):
    copies = []
    for n, group in enumerate(groups):
        rows = weights.shape[2]
        copies.append(
            [
                pltpu.make_async_copy(
                    weights.at[j, group], slabs.at[n, j * rows : (j + 1) * rows], sems.at[n, j]
                )
                for j in range(SEQ)
            ]
        )
        for copy in copies[-1]:
            copy.start()
    return copies


def slab_scratch(count, weights):
    _, _, rows, columns = weights.shape
    return [
        pltpu.VMEM((count, SEQ * rows, columns), BF16),
        pltpu.SemaphoreType.DMA((count, SEQ)),
    ]


def extra_rows(gain, offset, group):
    tiles = []
    for j in range(SEQ):
        here = pl.ds(j * CLASSES + group, 1)
        ratio = offset[here] / gain[here]
        high = ratio.astype(BF16).astype(F32)
        row = lax.broadcasted_iota(jnp.int32, (AUX, HEAD_DIM), 0)
        tile = jnp.where(row == 0, 1.0, 0.0)
        tile = jnp.where(row == 1, jnp.broadcast_to(high, tile.shape), tile)
        tile = jnp.where(row == 2, jnp.broadcast_to(ratio - high, tile.shape), tile)
        tiles.append(tile.astype(BF16))
    return jnp.concatenate(tiles, axis=1)


def product_of(blocks, copies, slab, gain, offset, group):
    left = jnp.concatenate([block[...] for block in blocks], axis=1)
    left = jnp.concatenate([left, extra_rows(gain, offset, group)], axis=0)
    for copy in copies:
        copy.wait()
    return jnp.dot(left, slab[...], preferred_element_type=F32)


def add_stats(blocks, pivot, before1, before2, sum1, sum2, rows=64):
    for t in range(0, POS, rows):
        here = slice(t, t + rows)
        centre, one, two = pivot[here], before1[here], before2[here]
        for block in blocks:
            away = block[here].astype(F32) - centre
            one = one + away
            two = two + away * away
        sum1[here] = one
        sum2[here] = two


def first_kernel(offsets, place, *refs):
    count = len(offsets)
    parts, refs = refs[:count], refs[count:]
    weights, gain, offset, acc, pivot, sum1, sum2, slabs, sems = refs
    groups = [lax.rem(place[0] + away + CLASSES, CLASSES) for away in offsets]
    copies = fetch(weights, groups, slabs, sems)
    lead = jnp.mean(parts[0][0].astype(F32), axis=1, keepdims=True)
    pivot[...] = jnp.broadcast_to(lead, (POS, HEAD_DIM))
    sum1[...] = jnp.zeros((POS, HEAD_DIM), F32)
    sum2[...] = jnp.zeros((POS, HEAD_DIM), F32)
    for n, part in enumerate(parts):
        blocks = [part.at[j] for j in range(SEQ)]
        product = product_of(blocks, copies[n], slabs.at[n], gain, offset, groups[n])
        if n == 0:
            acc[...] = product
        else:
            acc[...] += product
        add_stats(blocks, pivot, sum1, sum2, sum1, sum2)


def more_kernel(offsets, place, *refs):
    count = len(offsets)
    parts, refs = refs[:count], refs[count:]
    acc, pivot, sum1, sum2, weights, gain, offset, acc_out, sum1_out, sum2_out, slabs, sems = refs
    groups = [lax.rem(place[0] + away + CLASSES, CLASSES) for away in offsets]
    copies = fetch(weights, groups, slabs, sems)
    for n, part in enumerate(parts):
        blocks = [part.at[j] for j in range(SEQ)]
        before = (acc, sum1, sum2) if n == 0 else (acc_out, sum1_out, sum2_out)
        product = product_of(blocks, copies[n], slabs.at[n], gain, offset, groups[n])
        acc_out[...] = before[0][...] + product
        add_stats(blocks, pivot, before[1], before[2], sum1_out, sum2_out)


def stage(kernel, offsets, place, parts, before, weights, gain, offset):
    vmem, here = pl.BlockSpec(memory_space=pltpu.VMEM), pl.BlockSpec(memory_space=pltpu.HBM)
    hidden = weights.shape[-1]
    stat = jax.ShapeDtypeStruct((POS, HEAD_DIM), F32)
    total = jax.ShapeDtypeStruct((POS + AUX, hidden), F32)
    out_shape = (total, stat, stat) if before else (total, stat, stat, stat)
    return pl.pallas_call(
        functools.partial(kernel, offsets),
        out_shape=out_shape,
        in_specs=[pl.BlockSpec(memory_space=pltpu.SMEM)]
        + [vmem] * (len(parts) + len(before))
        + [here, vmem, vmem],
        out_specs=(vmem,) * len(out_shape),
        scratch_shapes=slab_scratch(len(parts), weights),
        compiler_params=pltpu.CompilerParams(vmem_limit_bytes=16 << 20),
        cost_estimate=pl.CostEstimate(
            flops=len(parts) << 28, bytes_accessed=len(parts) << 20, transcendentals=0
        ),
        name="stage",
    )(place, *parts, *before, weights, gain, offset)


def last_kernel(place, *refs):
    acc, pivot, sum1, sum2, part, weights, gain, offset, bias, out, one, two, slabs, sems = refs
    group = lax.rem(place[0] + 4, CLASSES)
    (copies,) = fetch(weights, [group], slabs, sems)
    blocks = [part.at[j] for j in range(SEQ)]
    add_stats(blocks, pivot, sum1, sum2, one, two)
    product = acc[...] + product_of(blocks, copies, slabs.at[0], gain, offset, group)
    mean1 = jnp.sum(one[...], axis=1, keepdims=True) * (1.0 / C)
    mean2 = jnp.sum(two[...], axis=1, keepdims=True) * (1.0 / C)
    centre = pivot[:, 0:1] + mean1
    spread = jnp.maximum(mean2 - mean1 * mean1, 0.0)
    scale = lax.rsqrt(spread + 1e-06)
    slope = product[POS : POS + 1]
    level = product[POS + 1 : POS + 2] + product[POS + 2 : POS + 3] + bias[...]
    project = scale * (product[0:POS] - centre * slope) + level
    out[...] = (0.5 * project * (1.0 + lax.erf(project * math.sqrt(0.5)))).astype(BF16)


def last(place, acc, stats, part, weights, gain, offset, bias):
    vmem, here = pl.BlockSpec(memory_space=pltpu.VMEM), pl.BlockSpec(memory_space=pltpu.HBM)
    hidden = weights.shape[-1]
    return pl.pallas_call(
        last_kernel,
        out_shape=jax.ShapeDtypeStruct((POS, hidden), BF16),
        in_specs=[pl.BlockSpec(memory_space=pltpu.SMEM)] + [vmem] * 5 + [here] + [vmem] * 3,
        out_specs=vmem,
        scratch_shapes=[pltpu.VMEM((POS, HEAD_DIM), F32)] * 2 + slab_scratch(1, weights),
        compiler_params=pltpu.CompilerParams(vmem_limit_bytes=16 << 20),
        cost_estimate=pl.CostEstimate(flops=1 << 28, bytes_accessed=7 << 20, transcendentals=1 << 18),
        name="last",
    )(place, acc, *stats, part, weights, gain, offset, bias)


def on_device(
    inputs,
    query_proj,
    key_proj,
    value_proj,
    depth_weight,
    depth_bias,
    norm_gain,
    norm_bias,
    expand_weight,
    expand_bias,
):
    seq, row, col = (lax.axis_index(axis) for axis in ("seq", "row", "col"))
    depth, hidden = expand_weight.shape
    gain, offset = (a.reshape(C // depth, depth) for a in (norm_gain, norm_bias))
    x, q, k, v = (a.reshape(POS, HEAD_DIM) for a in (inputs, query_proj, key_proj, value_proj))
    x, q, k, v = (pltpu.with_memory_space_constraint(a, pltpu.HBM) for a in (x, q, k, v))
    mine = (seq * CLASSES + row).astype(jnp.int32).reshape(1)
    held = (pltpu.with_memory_space_constraint(a, pltpu.HBM) for a in (expand_weight, gain))
    qx, lower = pack(k, v, q, x)
    above = shift(lower, "seq", 1)
    kv, upper, scaled = scale(mine, k, v, q, x, *held)
    below, far = shift(upper, "seq", -1), shift(kv, "seq", 2)
    weights = lax.all_gather(scaled, ("seq", "row"), axis=0, tiled=True)
    weights = weights.reshape(SEQ, CLASSES, depth, hidden)
    weights = pltpu.with_memory_space_constraint(weights, pltpu.HBM)
    gain, offset = gain.astype(F32), offset.astype(F32)
    taps = depth_weight.astype(F32).reshape(KERNEL * KERNEL, HEAD_DIM)
    bias = depth_bias.astype(F32).reshape(1, HEAD_DIM)
    begun = near(kv, qx, above, below)
    residual, convolved = attend(
        seq.astype(jnp.int32).reshape(1), qx, above, below, far, begun, taps, bias
    )

    strides = [[i + CLASSES * j for j in range(SEQ)] for i in range(CLASSES)]
    own = lax.all_gather(convolved, "col", axis=0, tiled=True, axis_index_groups=strides)
    own = own.reshape(SEQ, POS, HEAD_DIM)
    pairs, up, down = [], own, own
    for _ in range(3):
        up, down = shift(up, "col", 1), shift(down, "col", -1)
        pairs.append((up, down))
    place = col.astype(jnp.int32).reshape(1)
    parts = (own, *pairs[0], *pairs[1])
    before = stage(first_kernel, (0, -1, 1, -2, 2), place, parts, (), weights, gain, offset)
    up, before = lax.optimization_barrier((up, before))
    pairs[2] = (up, down)
    up = shift(up, "col", 1)
    acc, *sums = stage(more_kernel, (-3, 3), place, pairs[2], before, weights, gain, offset)
    pivot = before[1]
    bias = expand_bias.astype(F32).reshape(1, hidden)
    out = last(place, acc, (pivot, *sums), up, weights, gain, offset, bias)
    return (
        residual.reshape(inputs.shape),
        out.reshape(inputs.shape[:3] + (hidden,)),
    )


def solution(mesh):
    return jax.shard_map(
        on_device,
        mesh=mesh,
        in_specs=(
            P("row", "seq", None, "col"),
            P("row", "seq", None, "col"),
            P("row", "seq", None, "col"),
            P("row", "seq", None, "col"),
            P(None, None, "col"),
            P("col"),
            P(),
            P(),
            P(("seq", "row"), "col"),
            P("col"),
        ),
        out_specs=(P("row", "seq", None, "col"), P("row", "seq", None, "col")),
        check_vma=False,
    )
```

```python
import functools
import math

import jax
import jax.numpy as jnp
from jax import lax
from jax.experimental import pallas as pl
from jax.experimental.pallas import tpu as pltpu
from jax.sharding import PartitionSpec as P

HEAD_DIM = 128
KERNEL = 7
MARGIN = KERNEL // 2
IMG_W = 64
ROWS = 8
POS = ROWS * IMG_W
EDGE = MARGIN * IMG_W
C = 4096
SEQ = 4
CLASSES = 8
LEFT = 8
F32 = jnp.float32
BF16 = jnp.bfloat16


def shift(array, axis, by):
    peers = lax.axis_size(axis)
    return lax.ppermute(array, axis, [(i, (i + by) % peers) for i in range(peers)])


def move(pairs, sems):
    copies = [pltpu.make_async_copy(a, b, sems.at[i]) for i, (a, b) in enumerate(pairs)]
    for copy in copies:
        copy.start()
    return copies


def message_moves(k, v, q, x, message, edge):
    return [
        (k, message.at[0:POS]),
        (v, message.at[POS : 2 * POS]),
        (q.at[edge], message.at[2 * POS : 2 * POS + EDGE]),
        (x.at[edge], message.at[2 * POS + EDGE : 2 * (POS + EDGE)]),
    ]


def pack_kernel(k, v, q, x, kvw, qx, lower, sems):
    own = [(q, qx.at[0:POS]), (x, qx.at[POS:])]
    edge = slice(POS - EDGE, POS)
    copies = move(own + message_moves(k, v, q, x, lower, edge), sems)
    lower[2 * (POS + EDGE) :] = kvw[2 * POS :]
    for copy in copies:
        copy.wait()


def pack(k, v, q, x, kvw):
    vmem, here = pl.BlockSpec(memory_space=pltpu.VMEM), pl.BlockSpec(memory_space=pltpu.HBM)
    size = kvw.shape[0] - 2 * POS
    return pl.pallas_call(
        pack_kernel,
        out_shape=(
            jax.ShapeDtypeStruct((2 * POS, HEAD_DIM), BF16),
            jax.ShapeDtypeStruct((2 * (POS + EDGE) + size, HEAD_DIM), BF16),
        ),
        in_specs=[here] * 4 + [vmem],
        out_specs=(vmem,) * 2,
        scratch_shapes=[pltpu.SemaphoreType.DMA((6,))],
        compiler_params=pltpu.CompilerParams(vmem_limit_bytes=8 << 20),
        name="pack",
    )(k, v, q, x, kvw)


def scale_kernel(place, k, v, q, x, weight_in, gain_in, kvw, upper, weight, gain, sems):
    pairs = [(weight_in, weight), (gain_in, gain), (k, kvw.at[0:POS]), (v, kvw.at[POS : 2 * POS])]
    copies = move(pairs + message_moves(k, v, q, x, upper, slice(0, EDGE)), sems)
    for copy in copies[:2]:
        copy.wait()
    depth = weight.shape[0]
    gains = gain[...].astype(F32)
    line = lax.broadcasted_iota(jnp.int32, gains.shape, 0) == place[0]
    mine = jnp.sum(jnp.where(line, gains, 0.0), axis=0, keepdims=True)
    mine = jnp.transpose(jnp.broadcast_to(mine, (depth, depth)))
    for c in range(0, weight.shape[1], depth):
        tile = (weight[:, c : c + depth].astype(F32) * mine).astype(BF16)
        kvw[2 * POS + c : 2 * POS + c + depth] = tile
        upper[2 * (POS + EDGE) + c : 2 * (POS + EDGE) + c + depth] = tile
    for copy in copies[2:]:
        copy.wait()


def scale(place, k, v, q, x, weight, gain):
    vmem, here = pl.BlockSpec(memory_space=pltpu.VMEM), pl.BlockSpec(memory_space=pltpu.HBM)
    size = weight.size // HEAD_DIM
    return pl.pallas_call(
        scale_kernel,
        out_shape=(
            jax.ShapeDtypeStruct((2 * POS + size, HEAD_DIM), BF16),
            jax.ShapeDtypeStruct((2 * (POS + EDGE) + size, HEAD_DIM), BF16),
        ),
        in_specs=[pl.BlockSpec(memory_space=pltpu.SMEM)] + [here] * 6,
        out_specs=(vmem,) * 2,
        scratch_shapes=[
            pltpu.VMEM(weight.shape, BF16),
            pltpu.VMEM(gain.shape, BF16),
            pltpu.SemaphoreType.DMA((8,)),
        ],
        compiler_params=pltpu.CompilerParams(vmem_limit_bytes=8 << 20),
        name="scale",
    )(place, k, v, q, x, weight, gain)


TALL = ROWS + 2 * MARGIN
TO_LOG2 = math.log2(math.e) / math.sqrt(HEAD_DIM)
TILE = 2 * IMG_W


def spread_rows(above, own, below, rows, at):
    rows[0:EDGE] = above[at : at + EDGE]
    rows[EDGE : EDGE + POS] = own
    rows[EDGE + POS :] = below[at : at + EDGE]


def weigh(queries, parts, peak):
    scores = [
        lax.dot_general(queries, part[0:POS], (((1,), (1,)), ((), ())), preferred_element_type=F32)
        for part in parts
    ]
    highest = jnp.max(functools.reduce(jnp.maximum, scores), axis=1, keepdims=True)
    if peak is not None:
        highest = jnp.maximum(highest, peak)
    weights = [jnp.exp2((score - highest) * TO_LOG2) for score in scores]
    total = jnp.sum(functools.reduce(jnp.add, weights), axis=1, keepdims=True)
    summed = functools.reduce(
        jnp.add,
        [
            jnp.dot(weight.astype(BF16), part[POS : 2 * POS], preferred_element_type=F32)
            for weight, part in zip(weights, parts)
        ],
    )
    return highest, total, summed


def near_kernel(kv, qx, above, below, summed_out, peak_out, total_out, qs):
    spread_rows(above, qx[0:POS], below, qs, 2 * POS)
    for t in range(TALL // 2):
        own = slice(t * TILE, (t + 1) * TILE)
        peak, total, summed = weigh(qs[own], (kv, above, below), None)
        summed_out[own] = summed
        peak_out[own] = jnp.broadcast_to(peak, summed.shape)
        total_out[own] = jnp.broadcast_to(total, summed.shape)


def near(kv, qx, above, below):
    vmem = pl.BlockSpec(memory_space=pltpu.VMEM)
    out = jax.ShapeDtypeStruct((POS + 2 * EDGE, HEAD_DIM), F32)
    flops = 3 * (POS + 2 * EDGE) * SEQ * POS * HEAD_DIM
    return pl.pallas_call(
        near_kernel,
        out_shape=(out,) * 3,
        in_specs=[vmem] * 4,
        out_specs=(vmem,) * 3,
        scratch_shapes=[pltpu.VMEM((POS + 2 * EDGE, HEAD_DIM), BF16)],
        compiler_params=pltpu.CompilerParams(vmem_limit_bytes=16 << 20),
        cost_estimate=pl.CostEstimate(flops=flops, bytes_accessed=3 << 20, transcendentals=2 << 20),
        name="near",
    )(kv, qx, above, below)


def attend_kernel(place, kvw, qx, above, below, far, summed_in, peak_in, total_in, taps, bias, *refs):
    res, conv, rows, qs, xs, image = refs
    size = kvw.shape[0] - 2 * POS
    edges = 2 * (POS + EDGE)
    sources = ((kvw, 2 * POS), (above, edges), (far, 2 * POS), (below, edges))
    for n, (part, at) in enumerate(sources):
        rows[n * size : (n + 1) * size] = part[at : at + size]
    spread_rows(above, qx[0:POS], below, qs, 2 * POS)
    spread_rows(above, qx[POS:], below, xs, 2 * POS + EDGE)
    tall = TALL
    blank = jnp.zeros((tall, 8, HEAD_DIM), F32)
    image[:, 0:LEFT, :] = blank
    image[:, LEFT + IMG_W : LEFT + IMG_W + 8, :] = blank
    for t in range(tall // 2):
        own = slice(t * TILE, (t + 1) * TILE)
        before = peak_in[own]
        peak, total, summed = weigh(qs[own], (far,), before[:, 0:1])
        factor = jnp.exp2((before - peak) * TO_LOG2)
        total = total_in[own] * factor + total
        summed = summed_in[own] * factor + summed
        out = (xs[own].astype(F32) + summed / total).astype(BF16).astype(F32)
        image[2 * t : 2 * t + 2, LEFT : LEFT + IMG_W, :] = out.reshape(2, IMG_W, HEAD_DIM)

    @pl.when(place[0] == 0)
    def _():
        image[0:MARGIN] = jnp.zeros((MARGIN, IMG_W + 16, HEAD_DIM), F32)

    @pl.when(place[0] == SEQ - 1)
    def _():
        image[tall - MARGIN :] = jnp.zeros((MARGIN, IMG_W + 16, HEAD_DIM), F32)

    for i in range(ROWS):
        res[i * IMG_W : (i + 1) * IMG_W] = image[MARGIN + i, LEFT : LEFT + IMG_W, :].astype(BF16)
    wide = 16
    for c0 in range(0, IMG_W, wide):
        sums = [jnp.broadcast_to(bias[...], (wide, HEAD_DIM)) for _ in range(ROWS)]
        for b in range(KERNEL):
            start = LEFT - MARGIN + b + c0
            columns = [image[r, start : start + wide, :] for r in range(tall)]
            for a in range(KERNEL):
                tap = taps[a * KERNEL + b : a * KERNEL + b + 1, :]
                for i in range(ROWS):
                    sums[i] = sums[i] + columns[i + a] * tap
        for i in range(ROWS):
            conv[i * IMG_W + c0 : i * IMG_W + c0 + wide] = sums[i].astype(BF16)


def attend(place, kvw, qx, above, below, far, begun, taps, bias):
    out = jax.ShapeDtypeStruct((POS, HEAD_DIM), BF16)
    rows = jax.ShapeDtypeStruct((SEQ * (kvw.shape[0] - 2 * POS), HEAD_DIM), BF16)
    vmem = pl.BlockSpec(memory_space=pltpu.VMEM)
    flops = (POS + 2 * EDGE) * SEQ * POS * HEAD_DIM
    return pl.pallas_call(
        attend_kernel,
        out_shape=(out, out, rows),
        in_specs=[pl.BlockSpec(memory_space=pltpu.SMEM)] + [vmem] * 10,
        out_specs=(vmem,) * 3,
        scratch_shapes=[
            pltpu.VMEM((POS + 2 * EDGE, HEAD_DIM), BF16),
            pltpu.VMEM((POS + 2 * EDGE, HEAD_DIM), BF16),
            pltpu.VMEM((TALL, IMG_W + 16, HEAD_DIM), F32),
        ],
        compiler_params=pltpu.CompilerParams(vmem_limit_bytes=16 << 20),
        cost_estimate=pl.CostEstimate(flops=flops, bytes_accessed=2 << 20, transcendentals=1 << 19),
        name="attend",
    )(place, kvw, qx, above, below, far, *begun, taps, bias)


AUX = 16


NEAR = (0, -1, 2, 1)
PIECES = 2 * len(NEAR)


def fetch(place, pieces, groups, slabs, sems):
    seq, row = place[1], place[2]
    depth = pieces[0].shape[2]
    starts = [pl.multiple_of(lax.rem(seq + by + SEQ, SEQ) * depth, depth) for by in NEAR]
    fetched = []
    for n, group in enumerate(groups):
        away = lax.rem(group // 2 - row // 2 + SEQ, SEQ)
        apart = lax.rem(group + row, 2)
        for i, piece in enumerate(pieces):
            copies = [
                pltpu.make_async_copy(
                    piece.at[m], slabs.at[n, :, pl.ds(start, depth)], sems.at[n, m]
                )
                for m, start in enumerate(starts)
            ]
            wanted = (away == NEAR[i % SEQ] % SEQ) & (apart == i // SEQ)

            @pl.when(wanted)
            def _():
                for copy in copies:
                    copy.start()

        fetched.append(copies)
    return fetched


def slab_scratch(count, pieces):
    _, tiles, depth, columns = pieces[0].shape
    return [
        pltpu.VMEM((count, tiles, SEQ * depth, columns), BF16),
        pltpu.SemaphoreType.DMA((count, SEQ)),
    ]


def extra_rows(gain, offset, group):
    tiles = []
    for j in range(SEQ):
        here = pl.ds(j * CLASSES + group, 1)
        ratio = offset[here] / gain[here]
        high = ratio.astype(BF16).astype(F32)
        row = lax.broadcasted_iota(jnp.int32, (AUX, HEAD_DIM), 0)
        tile = jnp.where(row == 0, 1.0, 0.0)
        tile = jnp.where(row == 1, jnp.broadcast_to(high, tile.shape), tile)
        tile = jnp.where(row == 2, jnp.broadcast_to(ratio - high, tile.shape), tile)
        tiles.append(tile.astype(BF16))
    return jnp.concatenate(tiles, axis=1)


def product_of(blocks, copies, slab, gain, offset, group):
    left = jnp.concatenate([block[...] for block in blocks], axis=1)
    left = jnp.concatenate([left, extra_rows(gain, offset, group)], axis=0)
    for copy in copies:
        copy.wait()
    right = jnp.concatenate([slab[i] for i in range(slab.shape[0])], axis=1)
    return jnp.dot(left, right, preferred_element_type=F32)


def add_stats(blocks, pivot, before1, before2, sum1, sum2, rows=64):
    for t in range(0, POS, rows):
        here = slice(t, t + rows)
        centre, one, two = pivot[here], before1[here], before2[here]
        for block in blocks:
            away = block[here].astype(F32) - centre
            one = one + away
            two = two + away * away
        sum1[here] = one
        sum2[here] = two


def first_kernel(offsets, place, *refs):
    count = len(offsets)
    parts, refs = refs[:count], refs[count:]
    pieces, refs = refs[:PIECES], refs[PIECES:]
    gain, offset, acc, pivot, sum1, sum2, slabs, sems = refs
    groups = [lax.rem(place[0] + away + CLASSES, CLASSES) for away in offsets]
    copies = fetch(place, pieces, groups, slabs, sems)
    lead = jnp.mean(parts[0][0].astype(F32), axis=1, keepdims=True)
    pivot[...] = jnp.broadcast_to(lead, (POS, HEAD_DIM))
    sum1[...] = jnp.zeros((POS, HEAD_DIM), F32)
    sum2[...] = jnp.zeros((POS, HEAD_DIM), F32)
    for n, part in enumerate(parts):
        blocks = [part.at[j] for j in range(SEQ)]
        product = product_of(blocks, copies[n], slabs.at[n], gain, offset, groups[n])
        if n == 0:
            acc[...] = product
        else:
            acc[...] += product
        add_stats(blocks, pivot, sum1, sum2, sum1, sum2)


def more_kernel(offsets, place, *refs):
    count = len(offsets)
    parts, refs = refs[:count], refs[count:]
    acc, pivot, sum1, sum2, *refs = refs
    pieces, refs = refs[:PIECES], refs[PIECES:]
    gain, offset, acc_out, sum1_out, sum2_out, slabs, sems = refs
    groups = [lax.rem(place[0] + away + CLASSES, CLASSES) for away in offsets]
    copies = fetch(place, pieces, groups, slabs, sems)
    for n, part in enumerate(parts):
        blocks = [part.at[j] for j in range(SEQ)]
        before = (acc, sum1, sum2) if n == 0 else (acc_out, sum1_out, sum2_out)
        product = product_of(blocks, copies[n], slabs.at[n], gain, offset, groups[n])
        acc_out[...] = before[0][...] + product
        add_stats(blocks, pivot, before[1], before[2], sum1_out, sum2_out)


def stage(kernel, offsets, place, parts, before, pieces, gain, offset):
    vmem, here = pl.BlockSpec(memory_space=pltpu.VMEM), pl.BlockSpec(memory_space=pltpu.HBM)
    hidden = pieces[0].shape[1] * pieces[0].shape[3]
    stat = jax.ShapeDtypeStruct((POS, HEAD_DIM), F32)
    total = jax.ShapeDtypeStruct((POS + AUX, hidden), F32)
    out_shape = (total, stat, stat) if before else (total, stat, stat, stat)
    return pl.pallas_call(
        functools.partial(kernel, offsets),
        out_shape=out_shape,
        in_specs=[pl.BlockSpec(memory_space=pltpu.SMEM)]
        + [vmem] * (len(parts) + len(before))
        + [here] * PIECES
        + [vmem] * 2,
        out_specs=(vmem,) * len(out_shape),
        scratch_shapes=slab_scratch(len(parts), pieces),
        compiler_params=pltpu.CompilerParams(vmem_limit_bytes=16 << 20),
        cost_estimate=pl.CostEstimate(
            flops=len(parts) << 28, bytes_accessed=len(parts) << 20, transcendentals=0
        ),
        name="stage",
    )(place, *parts, *before, *pieces, gain, offset)


def last_kernel(place, *refs):
    acc, pivot, sum1, sum2, part, *refs = refs
    pieces, refs = refs[:PIECES], refs[PIECES:]
    gain, offset, bias, out, one, two, slabs, sems = refs
    group = lax.rem(place[0] + 4, CLASSES)
    (copies,) = fetch(place, pieces, [group], slabs, sems)
    blocks = [part.at[j] for j in range(SEQ)]
    add_stats(blocks, pivot, sum1, sum2, one, two)
    product = acc[...] + product_of(blocks, copies, slabs.at[0], gain, offset, group)
    mean1 = jnp.sum(one[...], axis=1, keepdims=True) * (1.0 / C)
    mean2 = jnp.sum(two[...], axis=1, keepdims=True) * (1.0 / C)
    centre = pivot[:, 0:1] + mean1
    spread = jnp.maximum(mean2 - mean1 * mean1, 0.0)
    scale = lax.rsqrt(spread + 1e-06)
    slope = product[POS : POS + 1]
    level = product[POS + 1 : POS + 2] + product[POS + 2 : POS + 3] + bias[...]
    project = scale * (product[0:POS] - centre * slope) + level
    out[...] = (0.5 * project * (1.0 + lax.erf(project * math.sqrt(0.5)))).astype(BF16)


def last(place, acc, stats, part, pieces, gain, offset, bias):
    vmem, here = pl.BlockSpec(memory_space=pltpu.VMEM), pl.BlockSpec(memory_space=pltpu.HBM)
    hidden = pieces[0].shape[1] * pieces[0].shape[3]
    return pl.pallas_call(
        last_kernel,
        out_shape=jax.ShapeDtypeStruct((POS, hidden), BF16),
        in_specs=[pl.BlockSpec(memory_space=pltpu.SMEM)] + [vmem] * 5 + [here] * PIECES + [vmem] * 3,
        out_specs=vmem,
        scratch_shapes=[pltpu.VMEM((POS, HEAD_DIM), F32)] * 2 + slab_scratch(1, pieces),
        compiler_params=pltpu.CompilerParams(vmem_limit_bytes=16 << 20),
        cost_estimate=pl.CostEstimate(flops=1 << 28, bytes_accessed=7 << 20, transcendentals=1 << 18),
        name="last",
    )(place, acc, *stats, part, *pieces, gain, offset, bias)


def on_device(
    inputs,
    query_proj,
    key_proj,
    value_proj,
    depth_weight,
    depth_bias,
    norm_gain,
    norm_bias,
    expand_weight,
    expand_bias,
):
    seq, row, col = (lax.axis_index(axis) for axis in ("seq", "row", "col"))
    depth, hidden = expand_weight.shape
    gain, offset = (a.reshape(C // depth, depth) for a in (norm_gain, norm_bias))
    x, q, k, v = (a.reshape(POS, HEAD_DIM) for a in (inputs, query_proj, key_proj, value_proj))
    x, q, k, v = (pltpu.with_memory_space_constraint(a, pltpu.HBM) for a in (x, q, k, v))
    mine = (seq * CLASSES + row).astype(jnp.int32).reshape(1)
    held = (pltpu.with_memory_space_constraint(a, pltpu.HBM) for a in (expand_weight, gain))
    kvw, upper = scale(mine, k, v, q, x, *held)
    below, far = shift(upper, "seq", -1), shift(kvw, "seq", 2)
    qx, lower = pack(k, v, q, x, kvw)
    above = shift(lower, "seq", 1)
    gain, offset = gain.astype(F32), offset.astype(F32)
    taps = depth_weight.astype(F32).reshape(KERNEL * KERNEL, HEAD_DIM)
    bias = depth_bias.astype(F32).reshape(1, HEAD_DIM)
    begun = near(kvw, qx, above, below)
    residual, convolved, rows = attend(
        seq.astype(jnp.int32).reshape(1), kvw, qx, above, below, far, begun, taps, bias
    )

    strides = [[i + CLASSES * j for j in range(SEQ)] for i in range(CLASSES)]
    own = lax.all_gather(convolved, "col", axis=0, tiled=True, axis_index_groups=strides)
    own = own.reshape(SEQ, POS, HEAD_DIM)
    _, rows = lax.optimization_barrier((own, rows))
    swap = [(i, i ^ 1) for i in range(lax.axis_size("row"))]
    along_y = [rows] + [shift(rows, "row", 2 * by) for by in (1, 2, -1)]
    pairs, up, down = [], own, own
    for n in range(3):
        up, down = shift(up, "col", 1), shift(down, "col", -1)
        if n == 0:
            down, *along_y[1:] = lax.optimization_barrier((down, *along_y[1:]))
        if n == 1:
            _, *along_y = lax.optimization_barrier((up, *along_y))
            other = [lax.ppermute(piece, "row", swap) for piece in along_y]
        pairs.append((up, down))
    depth_tiles = (SEQ, hidden // HEAD_DIM, depth, HEAD_DIM)
    pieces = [
        pltpu.with_memory_space_constraint(a.reshape(depth_tiles), pltpu.HBM)
        for a in along_y + other
    ]
    place = jnp.stack([col, seq, row]).astype(jnp.int32)
    parts = (own, *pairs[0], *pairs[1])
    before = stage(first_kernel, (0, -1, 1, -2, 2), place, parts, (), pieces, gain, offset)
    up = shift(up, "col", 1)
    acc, *sums = stage(more_kernel, (-3, 3), place, pairs[2], before, pieces, gain, offset)
    pivot = before[1]
    bias = expand_bias.astype(F32).reshape(1, hidden)
    out = last(place, acc, (pivot, *sums), up, pieces, gain, offset, bias)
    return (
        residual.reshape(inputs.shape),
        out.reshape(inputs.shape[:3] + (hidden,)),
    )


def solution(mesh):
    return jax.shard_map(
        on_device,
        mesh=mesh,
        in_specs=(
            P("row", "seq", None, "col"),
            P("row", "seq", None, "col"),
            P("row", "seq", None, "col"),
            P("row", "seq", None, "col"),
            P(None, None, "col"),
            P("col"),
            P(),
            P(),
            P(("seq", "row"), "col"),
            P("col"),
        ),
        out_specs=(P("row", "seq", None, "col"), P("row", "seq", None, "col")),
        check_vma=False,
    )
```

```python
import functools
import math

import jax
import jax.numpy as jnp
from jax import lax
from jax.experimental import pallas as pl
from jax.experimental.pallas import tpu as pltpu
from jax.sharding import PartitionSpec as P

HEAD_DIM = 128
KERNEL = 7
MARGIN = KERNEL // 2
IMG_W = 64
ROWS = 8
POS = ROWS * IMG_W
EDGE = MARGIN * IMG_W
C = 4096
SEQ = 4
CLASSES = 8
LEFT = 8
F32 = jnp.float32
BF16 = jnp.bfloat16


def shift(array, axis, by):
    peers = lax.axis_size(axis)
    return lax.ppermute(array, axis, [(i, (i + by) % peers) for i in range(peers)])


def move(pairs, sems):
    copies = [pltpu.make_async_copy(a, b, sems.at[i]) for i, (a, b) in enumerate(pairs)]
    for copy in copies:
        copy.start()
    return copies


def message_moves(k, v, q, x, message, edge):
    return [
        (k, message.at[0:POS]),
        (v, message.at[POS : 2 * POS]),
        (q.at[edge], message.at[2 * POS : 2 * POS + EDGE]),
        (x.at[edge], message.at[2 * POS + EDGE : 2 * (POS + EDGE)]),
    ]


def pack_kernel(k, v, q, x, kvw, qx, lower, sems):
    own = [(q, qx.at[0:POS]), (x, qx.at[POS:])]
    edge = slice(POS - EDGE, POS)
    copies = move(own + message_moves(k, v, q, x, lower, edge), sems)
    lower[2 * (POS + EDGE) :] = kvw[2 * POS :]
    for copy in copies:
        copy.wait()


def pack(k, v, q, x, kvw):
    vmem, here = pl.BlockSpec(memory_space=pltpu.VMEM), pl.BlockSpec(memory_space=pltpu.HBM)
    size = kvw.shape[0] - 2 * POS
    return pl.pallas_call(
        pack_kernel,
        out_shape=(
            jax.ShapeDtypeStruct((2 * POS, HEAD_DIM), BF16),
            jax.ShapeDtypeStruct((2 * (POS + EDGE) + size, HEAD_DIM), BF16),
        ),
        in_specs=[here] * 4 + [vmem],
        out_specs=(vmem,) * 2,
        scratch_shapes=[pltpu.SemaphoreType.DMA((6,))],
        compiler_params=pltpu.CompilerParams(vmem_limit_bytes=8 << 20),
        name="pack",
    )(k, v, q, x, kvw)


def scale_kernel(place, k, v, q, x, weight_in, gain_in, kvw, upper, weight, gain, sems):
    pairs = [(weight_in, weight), (gain_in, gain), (k, kvw.at[0:POS]), (v, kvw.at[POS : 2 * POS])]
    copies = move(pairs + message_moves(k, v, q, x, upper, slice(0, EDGE)), sems)
    for copy in copies[:2]:
        copy.wait()
    depth = weight.shape[0]
    gains = gain[...].astype(F32)
    line = lax.broadcasted_iota(jnp.int32, gains.shape, 0) == place[0]
    mine = jnp.sum(jnp.where(line, gains, 0.0), axis=0, keepdims=True)
    mine = jnp.transpose(jnp.broadcast_to(mine, (depth, depth)))
    for c in range(0, weight.shape[1], depth):
        tile = (weight[:, c : c + depth].astype(F32) * mine).astype(BF16)
        kvw[2 * POS + c : 2 * POS + c + depth] = tile
        upper[2 * (POS + EDGE) + c : 2 * (POS + EDGE) + c + depth] = tile
    for copy in copies[2:]:
        copy.wait()


def scale(place, k, v, q, x, weight, gain):
    vmem, here = pl.BlockSpec(memory_space=pltpu.VMEM), pl.BlockSpec(memory_space=pltpu.HBM)
    size = weight.size // HEAD_DIM
    return pl.pallas_call(
        scale_kernel,
        out_shape=(
            jax.ShapeDtypeStruct((2 * POS + size, HEAD_DIM), BF16),
            jax.ShapeDtypeStruct((2 * (POS + EDGE) + size, HEAD_DIM), BF16),
        ),
        in_specs=[pl.BlockSpec(memory_space=pltpu.SMEM)] + [here] * 6,
        out_specs=(vmem,) * 2,
        scratch_shapes=[
            pltpu.VMEM(weight.shape, BF16),
            pltpu.VMEM(gain.shape, BF16),
            pltpu.SemaphoreType.DMA((8,)),
        ],
        compiler_params=pltpu.CompilerParams(vmem_limit_bytes=8 << 20),
        name="scale",
    )(place, k, v, q, x, weight, gain)


TALL = ROWS + 2 * MARGIN
TO_LOG2 = math.log2(math.e) / math.sqrt(HEAD_DIM)
TILE = 2 * IMG_W


def spread_rows(above, own, below, rows, at):
    rows[0:EDGE] = above[at : at + EDGE]
    rows[EDGE : EDGE + POS] = own
    rows[EDGE + POS :] = below[at : at + EDGE]


def weigh(queries, parts, peak):
    scores = [
        lax.dot_general(queries, part[0:POS], (((1,), (1,)), ((), ())), preferred_element_type=F32)
        for part in parts
    ]
    highest = jnp.max(functools.reduce(jnp.maximum, scores), axis=1, keepdims=True)
    if peak is not None:
        highest = jnp.maximum(highest, peak)
    weights = [jnp.exp2((score - highest) * TO_LOG2) for score in scores]
    total = jnp.sum(functools.reduce(jnp.add, weights), axis=1, keepdims=True)
    summed = functools.reduce(
        jnp.add,
        [
            jnp.dot(weight.astype(BF16), part[POS : 2 * POS], preferred_element_type=F32)
            for weight, part in zip(weights, parts)
        ],
    )
    return highest, total, summed


def near_kernel(kv, qx, above, below, summed_out, peak_out, total_out, qs):
    spread_rows(above, qx[0:POS], below, qs, 2 * POS)
    for t in range(TALL // 2):
        own = slice(t * TILE, (t + 1) * TILE)
        peak, total, summed = weigh(qs[own], (kv, above, below), None)
        summed_out[own] = summed
        peak_out[own] = jnp.broadcast_to(peak, summed.shape)
        total_out[own] = jnp.broadcast_to(total, summed.shape)


def near(kv, qx, above, below):
    vmem = pl.BlockSpec(memory_space=pltpu.VMEM)
    out = jax.ShapeDtypeStruct((POS + 2 * EDGE, HEAD_DIM), F32)
    flops = 3 * (POS + 2 * EDGE) * SEQ * POS * HEAD_DIM
    return pl.pallas_call(
        near_kernel,
        out_shape=(out,) * 3,
        in_specs=[vmem] * 4,
        out_specs=(vmem,) * 3,
        scratch_shapes=[pltpu.VMEM((POS + 2 * EDGE, HEAD_DIM), BF16)],
        compiler_params=pltpu.CompilerParams(vmem_limit_bytes=16 << 20),
        cost_estimate=pl.CostEstimate(flops=flops, bytes_accessed=3 << 20, transcendentals=2 << 20),
        name="near",
    )(kv, qx, above, below)


def attend_kernel(place, kvw, qx, above, below, far, summed_in, peak_in, total_in, taps, bias, *refs):
    res, conv, rows, qs, xs, image = refs
    size = kvw.shape[0] - 2 * POS
    edges = 2 * (POS + EDGE)
    sources = ((kvw, 2 * POS), (above, edges), (far, 2 * POS), (below, edges))
    for n, (part, at) in enumerate(sources):
        rows[n * size : (n + 1) * size] = part[at : at + size]
    spread_rows(above, qx[0:POS], below, qs, 2 * POS)
    spread_rows(above, qx[POS:], below, xs, 2 * POS + EDGE)
    tall = TALL
    blank = jnp.zeros((tall, 8, HEAD_DIM), F32)
    image[:, 0:LEFT, :] = blank
    image[:, LEFT + IMG_W : LEFT + IMG_W + 8, :] = blank
    for t in range(tall // 2):
        own = slice(t * TILE, (t + 1) * TILE)
        before = peak_in[own]
        peak, total, summed = weigh(qs[own], (far,), before[:, 0:1])
        factor = jnp.exp2((before - peak) * TO_LOG2)
        total = total_in[own] * factor + total
        summed = summed_in[own] * factor + summed
        out = (xs[own].astype(F32) + summed / total).astype(BF16).astype(F32)
        image[2 * t : 2 * t + 2, LEFT : LEFT + IMG_W, :] = out.reshape(2, IMG_W, HEAD_DIM)

    @pl.when(place[0] == 0)
    def _():
        image[0:MARGIN] = jnp.zeros((MARGIN, IMG_W + 16, HEAD_DIM), F32)

    @pl.when(place[0] == SEQ - 1)
    def _():
        image[tall - MARGIN :] = jnp.zeros((MARGIN, IMG_W + 16, HEAD_DIM), F32)

    for i in range(ROWS):
        res[i * IMG_W : (i + 1) * IMG_W] = image[MARGIN + i, LEFT : LEFT + IMG_W, :].astype(BF16)
    wide = 16
    for c0 in range(0, IMG_W, wide):
        sums = [jnp.broadcast_to(bias[...], (wide, HEAD_DIM)) for _ in range(ROWS)]
        for b in range(KERNEL):
            start = LEFT - MARGIN + b + c0
            columns = [image[r, start : start + wide, :] for r in range(tall)]
            for a in range(KERNEL):
                tap = taps[a * KERNEL + b : a * KERNEL + b + 1, :]
                for i in range(ROWS):
                    sums[i] = sums[i] + columns[i + a] * tap
        for i in range(ROWS):
            conv[i * IMG_W + c0 : i * IMG_W + c0 + wide] = sums[i].astype(BF16)


def attend(place, kvw, qx, above, below, far, begun, taps, bias):
    out = jax.ShapeDtypeStruct((POS, HEAD_DIM), BF16)
    rows = jax.ShapeDtypeStruct((SEQ * (kvw.shape[0] - 2 * POS), HEAD_DIM), BF16)
    vmem = pl.BlockSpec(memory_space=pltpu.VMEM)
    flops = (POS + 2 * EDGE) * SEQ * POS * HEAD_DIM
    return pl.pallas_call(
        attend_kernel,
        out_shape=(out, out, rows),
        in_specs=[pl.BlockSpec(memory_space=pltpu.SMEM)] + [vmem] * 10,
        out_specs=(vmem,) * 3,
        scratch_shapes=[
            pltpu.VMEM((POS + 2 * EDGE, HEAD_DIM), BF16),
            pltpu.VMEM((POS + 2 * EDGE, HEAD_DIM), BF16),
            pltpu.VMEM((TALL, IMG_W + 16, HEAD_DIM), F32),
        ],
        compiler_params=pltpu.CompilerParams(vmem_limit_bytes=16 << 20),
        cost_estimate=pl.CostEstimate(flops=flops, bytes_accessed=2 << 20, transcendentals=1 << 19),
        name="attend",
    )(place, kvw, qx, above, below, far, *begun, taps, bias)


AUX = 16


NEAR = (0, -1, 2, 1)
PIECES = 2 * len(NEAR)


def fetch(place, pieces, groups, targets, sems):
    seq, row = place[1], place[2]
    depth = pieces[0].shape[2]
    starts = [pl.multiple_of(lax.rem(seq + by + SEQ, SEQ) * depth, depth) for by in NEAR]
    fetched = []
    for n, group in enumerate(groups):
        away = lax.rem(group // 2 - row // 2 + SEQ, SEQ)
        apart = lax.rem(group + row, 2)
        for i, piece in enumerate(pieces):
            copies = [
                pltpu.make_async_copy(
                    piece.at[m], targets[n].at[:, pl.ds(start, depth)], sems.at[n, m]
                )
                for m, start in enumerate(starts)
            ]
            wanted = (away == NEAR[i % SEQ] % SEQ) & (apart == i // SEQ)

            @pl.when(wanted)
            def _():
                for copy in copies:
                    copy.start()

        fetched.append(copies)
    return fetched


def slab_scratch(count, pieces):
    _, tiles, depth, columns = pieces[0].shape
    return [
        pltpu.VMEM((count, tiles, SEQ * depth, columns), BF16),
        pltpu.SemaphoreType.DMA((count + 1, SEQ)),
    ]


def extra_rows(gain, offset, group):
    tiles = []
    for j in range(SEQ):
        here = pl.ds(j * CLASSES + group, 1)
        ratio = offset[here] / gain[here]
        high = ratio.astype(BF16).astype(F32)
        row = lax.broadcasted_iota(jnp.int32, (AUX, HEAD_DIM), 0)
        tile = jnp.where(row == 0, 1.0, 0.0)
        tile = jnp.where(row == 1, jnp.broadcast_to(high, tile.shape), tile)
        tile = jnp.where(row == 2, jnp.broadcast_to(ratio - high, tile.shape), tile)
        tiles.append(tile.astype(BF16))
    return jnp.concatenate(tiles, axis=1)


def product_of(blocks, copies, slab, gain, offset, group):
    left = jnp.concatenate([block[...] for block in blocks], axis=1)
    left = jnp.concatenate([left, extra_rows(gain, offset, group)], axis=0)
    for copy in copies:
        copy.wait()
    right = jnp.concatenate([slab[i] for i in range(slab.shape[0])], axis=1)
    return jnp.dot(left, right, preferred_element_type=F32)


def add_stats(blocks, pivot, before1, before2, sum1, sum2, rows=64):
    for t in range(0, POS, rows):
        here = slice(t, t + rows)
        centre, one, two = pivot[here], before1[here], before2[here]
        for block in blocks:
            away = block[here].astype(F32) - centre
            one = one + away
            two = two + away * away
        sum1[here] = one
        sum2[here] = two


def first_kernel(offsets, place, *refs):
    count = len(offsets)
    parts, refs = refs[:count], refs[count:]
    pieces, refs = refs[:PIECES], refs[PIECES:]
    gain, offset, acc, pivot, sum1, sum2, slabs, sems = refs
    groups = [lax.rem(place[0] + away + CLASSES, CLASSES) for away in offsets]
    copies = fetch(place, pieces, groups, [slabs.at[n] for n in range(count)], sems)
    lead = jnp.mean(parts[0][0].astype(F32), axis=1, keepdims=True)
    pivot[...] = jnp.broadcast_to(lead, (POS, HEAD_DIM))
    sum1[...] = jnp.zeros((POS, HEAD_DIM), F32)
    sum2[...] = jnp.zeros((POS, HEAD_DIM), F32)
    for n, part in enumerate(parts):
        blocks = [part.at[j] for j in range(SEQ)]
        product = product_of(blocks, copies[n], slabs.at[n], gain, offset, groups[n])
        if n == 0:
            acc[...] = product
        else:
            acc[...] += product
        add_stats(blocks, pivot, sum1, sum2, sum1, sum2)


def more_kernel(offsets, place, *refs):
    count = len(offsets)
    parts, refs = refs[:count], refs[count:]
    acc, pivot, sum1, sum2, *refs = refs
    pieces, refs = refs[:PIECES], refs[PIECES:]
    gain, offset, acc_out, sum1_out, sum2_out, slab_out, slabs, sems = refs
    groups = [lax.rem(place[0] + away + CLASSES, CLASSES) for away in (*offsets, SEQ)]
    targets = [slabs.at[n] for n in range(count)] + [slab_out]
    copies = fetch(place, pieces, groups, targets, sems)
    for n, part in enumerate(parts):
        blocks = [part.at[j] for j in range(SEQ)]
        before = (acc, sum1, sum2) if n == 0 else (acc_out, sum1_out, sum2_out)
        product = product_of(blocks, copies[n], slabs.at[n], gain, offset, groups[n])
        acc_out[...] = before[0][...] + product
        add_stats(blocks, pivot, before[1], before[2], sum1_out, sum2_out)
    for copy in copies[count]:
        copy.wait()


def stage(kernel, offsets, place, parts, before, pieces, gain, offset):
    vmem, here = pl.BlockSpec(memory_space=pltpu.VMEM), pl.BlockSpec(memory_space=pltpu.HBM)
    hidden = pieces[0].shape[1] * pieces[0].shape[3]
    stat = jax.ShapeDtypeStruct((POS, HEAD_DIM), F32)
    total = jax.ShapeDtypeStruct((POS + AUX, hidden), F32)
    _, tiles, depth, columns = pieces[0].shape
    slab = jax.ShapeDtypeStruct((tiles, SEQ * depth, columns), BF16)
    out_shape = (total, stat, stat, slab) if before else (total, stat, stat, stat)
    return pl.pallas_call(
        functools.partial(kernel, offsets),
        out_shape=out_shape,
        in_specs=[pl.BlockSpec(memory_space=pltpu.SMEM)]
        + [vmem] * (len(parts) + len(before))
        + [here] * PIECES
        + [vmem] * 2,
        out_specs=(vmem,) * len(out_shape),
        scratch_shapes=slab_scratch(len(parts), pieces),
        compiler_params=pltpu.CompilerParams(vmem_limit_bytes=16 << 20),
        cost_estimate=pl.CostEstimate(
            flops=len(parts) << 28, bytes_accessed=len(parts) << 20, transcendentals=0
        ),
        name="stage",
    )(place, *parts, *before, *pieces, gain, offset)


def last_kernel(place, *refs):
    acc, pivot, sum1, sum2, part, slab, gain, offset, bias, out, one, two = refs
    group = lax.rem(place[0] + SEQ, CLASSES)
    blocks = [part.at[j] for j in range(SEQ)]
    add_stats(blocks, pivot, sum1, sum2, one, two)
    product = acc[...] + product_of(blocks, (), slab, gain, offset, group)
    mean1 = jnp.sum(one[...], axis=1, keepdims=True) * (1.0 / C)
    mean2 = jnp.sum(two[...], axis=1, keepdims=True) * (1.0 / C)
    centre = pivot[:, 0:1] + mean1
    spread = jnp.maximum(mean2 - mean1 * mean1, 0.0)
    scale = lax.rsqrt(spread + 1e-06)
    slope = product[POS : POS + 1]
    level = product[POS + 1 : POS + 2] + product[POS + 2 : POS + 3] + bias[...]
    project = scale * (product[0:POS] - centre * slope) + level
    out[...] = (0.5 * project * (1.0 + lax.erf(project * math.sqrt(0.5)))).astype(BF16)


def last(place, acc, stats, part, slab, gain, offset, bias):
    vmem = pl.BlockSpec(memory_space=pltpu.VMEM)
    return pl.pallas_call(
        last_kernel,
        out_shape=jax.ShapeDtypeStruct((POS, bias.shape[1]), BF16),
        in_specs=[pl.BlockSpec(memory_space=pltpu.SMEM)] + [vmem] * 9,
        out_specs=vmem,
        scratch_shapes=[pltpu.VMEM((POS, HEAD_DIM), F32)] * 2,
        compiler_params=pltpu.CompilerParams(vmem_limit_bytes=16 << 20),
        cost_estimate=pl.CostEstimate(flops=1 << 28, bytes_accessed=4 << 20, transcendentals=1 << 18),
        name="last",
    )(place, acc, *stats, part, slab, gain, offset, bias)


def on_device(
    inputs,
    query_proj,
    key_proj,
    value_proj,
    depth_weight,
    depth_bias,
    norm_gain,
    norm_bias,
    expand_weight,
    expand_bias,
):
    seq, row, col = (lax.axis_index(axis) for axis in ("seq", "row", "col"))
    depth, hidden = expand_weight.shape
    gain, offset = (a.reshape(C // depth, depth) for a in (norm_gain, norm_bias))
    x, q, k, v = (a.reshape(POS, HEAD_DIM) for a in (inputs, query_proj, key_proj, value_proj))
    x, q, k, v = (pltpu.with_memory_space_constraint(a, pltpu.HBM) for a in (x, q, k, v))
    mine = (seq * CLASSES + row).astype(jnp.int32).reshape(1)
    held = (pltpu.with_memory_space_constraint(a, pltpu.HBM) for a in (expand_weight, gain))
    kvw, upper = scale(mine, k, v, q, x, *held)
    below, far = shift(upper, "seq", -1), shift(kvw, "seq", 2)
    qx, lower = pack(k, v, q, x, kvw)
    above = shift(lower, "seq", 1)
    gain, offset = gain.astype(F32), offset.astype(F32)
    taps = depth_weight.astype(F32).reshape(KERNEL * KERNEL, HEAD_DIM)
    bias = depth_bias.astype(F32).reshape(1, HEAD_DIM)
    begun = near(kvw, qx, above, below)
    residual, convolved, rows = attend(
        seq.astype(jnp.int32).reshape(1), kvw, qx, above, below, far, begun, taps, bias
    )

    strides = [[i + CLASSES * j for j in range(SEQ)] for i in range(CLASSES)]
    own = lax.all_gather(convolved, "col", axis=0, tiled=True, axis_index_groups=strides)
    own = own.reshape(SEQ, POS, HEAD_DIM)
    along_y = [rows] + [shift(rows, "row", 2 * by) for by in (1, 2, -1)]
    own, *along_y = lax.optimization_barrier((own, *along_y))
    swap = [(i, i ^ 1) for i in range(lax.axis_size("row"))]
    other, pairs, up, down = [], [], own, own
    for n in range(3):
        up, down = shift(up, "col", 1), shift(down, "col", -1)
        if n:
            two = [lax.ppermute(piece, "row", swap) for piece in along_y[2 * n - 2 : 2 * n]]
            down, *two = lax.optimization_barrier((down, *two))
            other += two
        pairs.append((up, down))
    depth_tiles = (SEQ, hidden // HEAD_DIM, depth, HEAD_DIM)
    pieces = [
        pltpu.with_memory_space_constraint(a.reshape(depth_tiles), pltpu.HBM)
        for a in along_y + other
    ]
    place = jnp.stack([col, seq, row]).astype(jnp.int32)
    parts = (own, *pairs[0], *pairs[1])
    before = stage(first_kernel, (0, -1, 1, -2, 2), place, parts, (), pieces, gain, offset)
    up = shift(up, "col", 1)
    acc, *sums, slab = stage(more_kernel, (-3, 3), place, pairs[2], before, pieces, gain, offset)
    pivot = before[1]
    bias = expand_bias.astype(F32).reshape(1, hidden)
    out = last(place, acc, (pivot, *sums), up, slab, gain, offset, bias)
    return (
        residual.reshape(inputs.shape),
        out.reshape(inputs.shape[:3] + (hidden,)),
    )


def solution(mesh):
    return jax.shard_map(
        on_device,
        mesh=mesh,
        in_specs=(
            P("row", "seq", None, "col"),
            P("row", "seq", None, "col"),
            P("row", "seq", None, "col"),
            P("row", "seq", None, "col"),
            P(None, None, "col"),
            P("col"),
            P(),
            P(),
            P(("seq", "row"), "col"),
            P("col"),
        ),
        out_specs=(P("row", "seq", None, "col"), P("row", "seq", None, "col")),
        check_vma=False,
    )
```

```python
import functools
import math

import jax
import jax.numpy as jnp
from jax import lax
from jax.experimental import pallas as pl
from jax.experimental.pallas import tpu as pltpu
from jax.sharding import PartitionSpec as P

HEAD_DIM = 128
KERNEL = 7
MARGIN = KERNEL // 2
IMG_W = 64
ROWS = 8
POS = ROWS * IMG_W
EDGE = MARGIN * IMG_W
C = 4096
SEQ = 4
CLASSES = 8
LEFT = 8
F32 = jnp.float32
BF16 = jnp.bfloat16


def shift(array, axis, by):
    peers = lax.axis_size(axis)
    return lax.ppermute(array, axis, [(i, (i + by) % peers) for i in range(peers)])


def move(pairs, sems):
    copies = [pltpu.make_async_copy(a, b, sems.at[i]) for i, (a, b) in enumerate(pairs)]
    for copy in copies:
        copy.start()
    return copies


def message_moves(k, v, q, x, message, edge):
    return [
        (k, message.at[0:POS]),
        (v, message.at[POS : 2 * POS]),
        (q.at[edge], message.at[2 * POS : 2 * POS + EDGE]),
        (x.at[edge], message.at[2 * POS + EDGE :]),
    ]


def pack_kernel(k, v, q, x, qx, lower, sems):
    own = [(q, qx.at[0:POS]), (x, qx.at[POS:])]
    edge = slice(POS - EDGE, POS)
    for copy in move(own + message_moves(k, v, q, x, lower, edge), sems):
        copy.wait()


def pack(k, v, q, x):
    vmem, here = pl.BlockSpec(memory_space=pltpu.VMEM), pl.BlockSpec(memory_space=pltpu.HBM)
    two = jax.ShapeDtypeStruct((2 * POS, HEAD_DIM), BF16)
    message = jax.ShapeDtypeStruct((2 * (POS + EDGE), HEAD_DIM), BF16)
    return pl.pallas_call(
        pack_kernel,
        out_shape=(two, message),
        in_specs=[here] * 4,
        out_specs=(vmem,) * 2,
        scratch_shapes=[pltpu.SemaphoreType.DMA((6,))],
        compiler_params=pltpu.CompilerParams(vmem_limit_bytes=8 << 20),
        name="pack",
    )(k, v, q, x)


def scale_kernel(place, k, v, q, x, weight_in, gain_in, kv, upper, scaled, weight, gain, sems):
    pairs = [(weight_in, weight), (gain_in, gain), (k, kv.at[0:POS]), (v, kv.at[POS:])]
    copies = move(pairs + message_moves(k, v, q, x, upper, slice(0, EDGE)), sems)
    for copy in copies[:2]:
        copy.wait()
    depth = weight.shape[0]
    gains = gain[...].astype(F32)
    line = lax.broadcasted_iota(jnp.int32, gains.shape, 0) == place[0]
    mine = jnp.sum(jnp.where(line, gains, 0.0), axis=0, keepdims=True)
    mine = jnp.transpose(jnp.broadcast_to(mine, (depth, depth)))
    for c in range(0, weight.shape[1], depth):
        scaled[:, c : c + depth] = (weight[:, c : c + depth].astype(F32) * mine).astype(BF16)
    for copy in copies[2:]:
        copy.wait()


def scale(place, k, v, q, x, weight, gain):
    vmem, here = pl.BlockSpec(memory_space=pltpu.VMEM), pl.BlockSpec(memory_space=pltpu.HBM)
    message = jax.ShapeDtypeStruct((2 * (POS + EDGE), HEAD_DIM), BF16)
    return pl.pallas_call(
        scale_kernel,
        out_shape=(
            jax.ShapeDtypeStruct((2 * POS, HEAD_DIM), BF16),
            message,
            jax.ShapeDtypeStruct(weight.shape, BF16),
        ),
        in_specs=[pl.BlockSpec(memory_space=pltpu.SMEM)] + [here] * 6,
        out_specs=(vmem,) * 3,
        scratch_shapes=[
            pltpu.VMEM(weight.shape, BF16),
            pltpu.VMEM(gain.shape, BF16),
            pltpu.SemaphoreType.DMA((8,)),
        ],
        compiler_params=pltpu.CompilerParams(vmem_limit_bytes=8 << 20),
        name="scale",
    )(place, k, v, q, x, weight, gain)


TALL = ROWS + 2 * MARGIN
TO_LOG2 = math.log2(math.e) / math.sqrt(HEAD_DIM)
TILE = 2 * IMG_W


def spread_rows(above, own, below, rows, at):
    rows[0:EDGE] = above[at : at + EDGE]
    rows[EDGE : EDGE + POS] = own
    rows[EDGE + POS :] = below[at : at + EDGE]


def weigh(queries, parts, peak):
    scores = [
        lax.dot_general(queries, part[0:POS], (((1,), (1,)), ((), ())), preferred_element_type=F32)
        for part in parts
    ]
    highest = jnp.max(functools.reduce(jnp.maximum, scores), axis=1, keepdims=True)
    if peak is not None:
        highest = jnp.maximum(highest, peak)
    weights = [jnp.exp2((score - highest) * TO_LOG2) for score in scores]
    total = jnp.sum(functools.reduce(jnp.add, weights), axis=1, keepdims=True)
    summed = functools.reduce(
        jnp.add,
        [
            jnp.dot(weight.astype(BF16), part[POS : 2 * POS], preferred_element_type=F32)
            for weight, part in zip(weights, parts)
        ],
    )
    return highest, total, summed


def near_kernel(kv, qx, above, below, summed_out, peak_out, total_out, qs):
    spread_rows(above, qx[0:POS], below, qs, 2 * POS)
    for t in range(TALL // 2):
        own = slice(t * TILE, (t + 1) * TILE)
        peak, total, summed = weigh(qs[own], (kv, above, below), None)
        summed_out[own] = summed
        peak_out[own] = jnp.broadcast_to(peak, summed.shape)
        total_out[own] = jnp.broadcast_to(total, summed.shape)


def near(kv, qx, above, below):
    vmem = pl.BlockSpec(memory_space=pltpu.VMEM)
    out = jax.ShapeDtypeStruct((POS + 2 * EDGE, HEAD_DIM), F32)
    flops = 3 * (POS + 2 * EDGE) * SEQ * POS * HEAD_DIM
    return pl.pallas_call(
        near_kernel,
        out_shape=(out,) * 3,
        in_specs=[vmem] * 4,
        out_specs=(vmem,) * 3,
        scratch_shapes=[pltpu.VMEM((POS + 2 * EDGE, HEAD_DIM), BF16)],
        compiler_params=pltpu.CompilerParams(vmem_limit_bytes=16 << 20),
        cost_estimate=pl.CostEstimate(flops=flops, bytes_accessed=3 << 20, transcendentals=2 << 20),
        name="near",
    )(kv, qx, above, below)


def attend_kernel(place, qx, above, below, far, summed_in, peak_in, total_in, taps, bias, res, conv, qs, xs, image):
    spread_rows(above, qx[0:POS], below, qs, 2 * POS)
    spread_rows(above, qx[POS:], below, xs, 2 * POS + EDGE)
    tall = TALL
    blank = jnp.zeros((tall, 8, HEAD_DIM), F32)
    image[:, 0:LEFT, :] = blank
    image[:, LEFT + IMG_W : LEFT + IMG_W + 8, :] = blank
    for t in range(tall // 2):
        own = slice(t * TILE, (t + 1) * TILE)
        before = peak_in[own]
        peak, total, summed = weigh(qs[own], (far,), before[:, 0:1])
        factor = jnp.exp2((before - peak) * TO_LOG2)
        total = total_in[own] * factor + total
        summed = summed_in[own] * factor + summed
        out = (xs[own].astype(F32) + summed / total).astype(BF16).astype(F32)
        image[2 * t : 2 * t + 2, LEFT : LEFT + IMG_W, :] = out.reshape(2, IMG_W, HEAD_DIM)

    @pl.when(place[0] == 0)
    def _():
        image[0:MARGIN] = jnp.zeros((MARGIN, IMG_W + 16, HEAD_DIM), F32)

    @pl.when(place[0] == SEQ - 1)
    def _():
        image[tall - MARGIN :] = jnp.zeros((MARGIN, IMG_W + 16, HEAD_DIM), F32)

    for i in range(ROWS):
        res[i * IMG_W : (i + 1) * IMG_W] = image[MARGIN + i, LEFT : LEFT + IMG_W, :].astype(BF16)
    wide = 16
    for c0 in range(0, IMG_W, wide):
        sums = [jnp.broadcast_to(bias[...], (wide, HEAD_DIM)) for _ in range(ROWS)]
        for b in range(KERNEL):
            start = LEFT - MARGIN + b + c0
            columns = [image[r, start : start + wide, :] for r in range(tall)]
            for a in range(KERNEL):
                tap = taps[a * KERNEL + b : a * KERNEL + b + 1, :]
                for i in range(ROWS):
                    sums[i] = sums[i] + columns[i + a] * tap
        for i in range(ROWS):
            conv[i, c0 : c0 + wide] = sums[i].astype(BF16)


def attend(place, qx, above, below, far, begun, taps, bias):
    out = jax.ShapeDtypeStruct((POS, HEAD_DIM), BF16)
    vmem = pl.BlockSpec(memory_space=pltpu.VMEM)
    flops = (POS + 2 * EDGE) * SEQ * POS * HEAD_DIM
    return pl.pallas_call(
        attend_kernel,
        out_shape=(out, jax.ShapeDtypeStruct((ROWS, IMG_W, HEAD_DIM), BF16)),
        in_specs=[pl.BlockSpec(memory_space=pltpu.SMEM)] + [vmem] * 9,
        out_specs=(vmem, vmem),
        scratch_shapes=[
            pltpu.VMEM((POS + 2 * EDGE, HEAD_DIM), BF16),
            pltpu.VMEM((POS + 2 * EDGE, HEAD_DIM), BF16),
            pltpu.VMEM((TALL, IMG_W + 16, HEAD_DIM), F32),
        ],
        compiler_params=pltpu.CompilerParams(vmem_limit_bytes=16 << 20),
        cost_estimate=pl.CostEstimate(flops=flops, bytes_accessed=2 << 20, transcendentals=1 << 19),
        name="attend",
    )(place, qx, above, below, far, *begun, taps, bias)


AUX = 16


def fetch(weights, groups, targets, sems):
    copies = []
    for n, group in enumerate(groups):
        rows = weights.shape[2]
        copies.append(
            [
                pltpu.make_async_copy(
                    weights.at[j, group], targets[n].at[j * rows : (j + 1) * rows], sems.at[n, j]
                )
                for j in range(SEQ)
            ]
        )
        for copy in copies[-1]:
            copy.start()
    return copies


def slab_scratch(count, weights):
    _, _, rows, columns = weights.shape
    return [
        pltpu.VMEM((count, SEQ * rows, columns), BF16),
        pltpu.SemaphoreType.DMA((count + 1, SEQ)),
    ]


def extra_rows(gain, offset, group):
    tiles = []
    for j in range(SEQ):
        here = pl.ds(j * CLASSES + group, 1)
        ratio = offset[here] / gain[here]
        high = ratio.astype(BF16).astype(F32)
        row = lax.broadcasted_iota(jnp.int32, (AUX, HEAD_DIM), 0)
        tile = jnp.where(row == 0, 1.0, 0.0)
        tile = jnp.where(row == 1, jnp.broadcast_to(high, tile.shape), tile)
        tile = jnp.where(row == 2, jnp.broadcast_to(ratio - high, tile.shape), tile)
        tiles.append(tile.astype(BF16))
    return jnp.concatenate(tiles, axis=1)


def product_of(blocks, copies, slab, gain, offset, group):
    left = jnp.concatenate([block[...] for block in blocks], axis=1)
    left = jnp.concatenate([left, extra_rows(gain, offset, group)], axis=0)
    for copy in copies:
        copy.wait()
    return jnp.dot(left, slab[...], preferred_element_type=F32)


def add_stats(blocks, pivot, before1, before2, sum1, sum2, rows=64):
    for t in range(0, POS, rows):
        here = slice(t, t + rows)
        centre, one, two = pivot[here], before1[here], before2[here]
        for block in blocks:
            away = block[here].astype(F32) - centre
            one = one + away
            two = two + away * away
        sum1[here] = one
        sum2[here] = two


def first_kernel(offsets, place, *refs):
    count = len(offsets)
    parts, refs = refs[:count], refs[count:]
    weights, gain, offset, acc, pivot, sum1, sum2, slabs, sems = refs
    groups = [lax.rem(place[0] + away + CLASSES, CLASSES) for away in offsets]
    copies = fetch(weights, groups, [slabs.at[n] for n in range(count)], sems)
    lead = jnp.mean(parts[0][0].astype(F32), axis=1, keepdims=True)
    pivot[...] = jnp.broadcast_to(lead, (POS, HEAD_DIM))
    sum1[...] = jnp.zeros((POS, HEAD_DIM), F32)
    sum2[...] = jnp.zeros((POS, HEAD_DIM), F32)
    for n, part in enumerate(parts):
        blocks = [part.at[j] for j in range(SEQ)]
        product = product_of(blocks, copies[n], slabs.at[n], gain, offset, groups[n])
        if n == 0:
            acc[...] = product
        else:
            acc[...] += product
        add_stats(blocks, pivot, sum1, sum2, sum1, sum2)


def more_kernel(offsets, place, *refs):
    count = len(offsets)
    parts, refs = refs[:count], refs[count:]
    acc, pivot, sum1, sum2, weights, gain, offset, *refs = refs
    acc_out, sum1_out, sum2_out, slab_out, slabs, sems = refs
    groups = [lax.rem(place[0] + away + CLASSES, CLASSES) for away in (*offsets, SEQ)]
    targets = [slabs.at[n] for n in range(count)] + [slab_out]
    copies = fetch(weights, groups, targets, sems)
    for n, part in enumerate(parts):
        blocks = [part.at[j] for j in range(SEQ)]
        before = (acc, sum1, sum2) if n == 0 else (acc_out, sum1_out, sum2_out)
        product = product_of(blocks, copies[n], slabs.at[n], gain, offset, groups[n])
        acc_out[...] = before[0][...] + product
        add_stats(blocks, pivot, before[1], before[2], sum1_out, sum2_out)
    for copy in copies[count]:
        copy.wait()


def stage(kernel, offsets, place, parts, before, weights, gain, offset):
    vmem, here = pl.BlockSpec(memory_space=pltpu.VMEM), pl.BlockSpec(memory_space=pltpu.HBM)
    hidden = weights.shape[-1]
    stat = jax.ShapeDtypeStruct((POS, HEAD_DIM), F32)
    total = jax.ShapeDtypeStruct((POS + AUX, hidden), F32)
    slab = jax.ShapeDtypeStruct((SEQ * weights.shape[2], hidden), BF16)
    out_shape = (total, stat, stat, slab) if before else (total, stat, stat, stat)
    return pl.pallas_call(
        functools.partial(kernel, offsets),
        out_shape=out_shape,
        in_specs=[pl.BlockSpec(memory_space=pltpu.SMEM)]
        + [vmem] * (len(parts) + len(before))
        + [here, vmem, vmem],
        out_specs=(vmem,) * len(out_shape),
        scratch_shapes=slab_scratch(len(parts), weights),
        compiler_params=pltpu.CompilerParams(vmem_limit_bytes=16 << 20),
        cost_estimate=pl.CostEstimate(
            flops=len(parts) << 28, bytes_accessed=len(parts) << 20, transcendentals=0
        ),
        name="stage",
    )(place, *parts, *before, weights, gain, offset)


def last_kernel(place, *refs):
    acc, pivot, sum1, sum2, part, slab, gain, offset, bias, out, one, two = refs
    group = lax.rem(place[0] + SEQ, CLASSES)
    blocks = [part.at[j] for j in range(SEQ)]
    add_stats(blocks, pivot, sum1, sum2, one, two)
    product = acc[...] + product_of(blocks, (), slab, gain, offset, group)
    mean1 = jnp.sum(one[...], axis=1, keepdims=True) * (1.0 / C)
    mean2 = jnp.sum(two[...], axis=1, keepdims=True) * (1.0 / C)
    centre = pivot[:, 0:1] + mean1
    spread = jnp.maximum(mean2 - mean1 * mean1, 0.0)
    scale = lax.rsqrt(spread + 1e-06)
    slope = product[POS : POS + 1]
    level = product[POS + 1 : POS + 2] + product[POS + 2 : POS + 3] + bias[...]
    project = scale * (product[0:POS] - centre * slope) + level
    out[...] = (0.5 * project * (1.0 + lax.erf(project * math.sqrt(0.5)))).astype(BF16)


def last(place, acc, stats, part, slab, gain, offset, bias):
    vmem = pl.BlockSpec(memory_space=pltpu.VMEM)
    return pl.pallas_call(
        last_kernel,
        out_shape=jax.ShapeDtypeStruct((POS, bias.shape[1]), BF16),
        in_specs=[pl.BlockSpec(memory_space=pltpu.SMEM)] + [vmem] * 9,
        out_specs=vmem,
        scratch_shapes=[pltpu.VMEM((POS, HEAD_DIM), F32)] * 2,
        compiler_params=pltpu.CompilerParams(vmem_limit_bytes=16 << 20),
        cost_estimate=pl.CostEstimate(flops=1 << 28, bytes_accessed=4 << 20, transcendentals=1 << 18),
        name="last",
    )(place, acc, *stats, part, slab, gain, offset, bias)


def on_device(
    inputs,
    query_proj,
    key_proj,
    value_proj,
    depth_weight,
    depth_bias,
    norm_gain,
    norm_bias,
    expand_weight,
    expand_bias,
):
    seq, row, col = (lax.axis_index(axis) for axis in ("seq", "row", "col"))
    depth, hidden = expand_weight.shape
    gain, offset = (a.reshape(C // depth, depth) for a in (norm_gain, norm_bias))
    x, q, k, v = (a.reshape(POS, HEAD_DIM) for a in (inputs, query_proj, key_proj, value_proj))
    x, q, k, v = (pltpu.with_memory_space_constraint(a, pltpu.HBM) for a in (x, q, k, v))
    mine = (seq * CLASSES + row).astype(jnp.int32).reshape(1)
    held = (pltpu.with_memory_space_constraint(a, pltpu.HBM) for a in (expand_weight, gain))
    qx, lower = pack(k, v, q, x)
    above = shift(lower, "seq", 1)
    kv, upper, scaled = scale(mine, k, v, q, x, *held)
    below, far = shift(upper, "seq", -1), shift(kv, "seq", 2)
    weights = lax.all_gather(scaled, ("seq", "row"), axis=0, tiled=True)
    weights = weights.reshape(SEQ, CLASSES, depth, hidden)
    weights = pltpu.with_memory_space_constraint(weights, pltpu.HBM)
    gain, offset = gain.astype(F32), offset.astype(F32)
    taps = depth_weight.astype(F32).reshape(KERNEL * KERNEL, HEAD_DIM)
    bias = depth_bias.astype(F32).reshape(1, HEAD_DIM)
    begun = near(kv, qx, above, below)
    residual, convolved = attend(
        seq.astype(jnp.int32).reshape(1), qx, above, below, far, begun, taps, bias
    )

    strides = [[i + CLASSES * j for j in range(SEQ)] for i in range(CLASSES)]
    own = lax.all_gather(convolved, "col", axis=0, tiled=True, axis_index_groups=strides)
    own = own.reshape(SEQ, POS, HEAD_DIM)
    pairs, up, down = [], own, own
    for _ in range(3):
        up, down = shift(up, "col", 1), shift(down, "col", -1)
        pairs.append((up, down))
    place = col.astype(jnp.int32).reshape(1)
    parts = (own, *pairs[0], *pairs[1])
    before = stage(first_kernel, (0, -1, 1, -2, 2), place, parts, (), weights, gain, offset)
    up, before = lax.optimization_barrier((up, before))
    pairs[2] = (up, down)
    up = shift(up, "col", 1)
    acc, *sums, slab = stage(more_kernel, (-3, 3), place, pairs[2], before, weights, gain, offset)
    pivot = before[1]
    bias = expand_bias.astype(F32).reshape(1, hidden)
    out = last(place, acc, (pivot, *sums), up, slab, gain, offset, bias)
    return (
        residual.reshape(inputs.shape),
        out.reshape(inputs.shape[:3] + (hidden,)),
    )


def solution(mesh):
    return jax.shard_map(
        on_device,
        mesh=mesh,
        in_specs=(
            P("row", "seq", None, "col"),
            P("row", "seq", None, "col"),
            P("row", "seq", None, "col"),
            P("row", "seq", None, "col"),
            P(None, None, "col"),
            P("col"),
            P(),
            P(),
            P(("seq", "row"), "col"),
            P("col"),
        ),
        out_specs=(P("row", "seq", None, "col"), P("row", "seq", None, "col")),
        check_vma=False,
    )
```

```python
import functools
import math

import jax
import jax.numpy as jnp
from jax import lax
from jax.experimental import pallas as pl
from jax.experimental.pallas import tpu as pltpu
from jax.sharding import PartitionSpec as P

HEAD_DIM = 128
KERNEL = 7
MARGIN = KERNEL // 2
IMG_W = 64
ROWS = 8
POS = ROWS * IMG_W
EDGE = MARGIN * IMG_W
C = 4096
SEQ = 4
CLASSES = 8
LEFT = 8
F32 = jnp.float32
BF16 = jnp.bfloat16


def shift(array, axis, by):
    peers = lax.axis_size(axis)
    return lax.ppermute(array, axis, [(i, (i + by) % peers) for i in range(peers)])


def move(pairs, sems):
    copies = [pltpu.make_async_copy(a, b, sems.at[i]) for i, (a, b) in enumerate(pairs)]
    for copy in copies:
        copy.start()
    return copies


def message_moves(k, v, q, x, message, edge):
    return [
        (k, message.at[0:POS]),
        (v, message.at[POS : 2 * POS]),
        (q.at[edge], message.at[2 * POS : 2 * POS + EDGE]),
        (x.at[edge], message.at[2 * POS + EDGE :]),
    ]


def pack_kernel(k, v, q, x, qx, lower, sems):
    own = [(q, qx.at[0:POS]), (x, qx.at[POS:])]
    edge = slice(POS - EDGE, POS)
    for copy in move(own + message_moves(k, v, q, x, lower, edge), sems):
        copy.wait()


def pack(k, v, q, x):
    vmem, here = pl.BlockSpec(memory_space=pltpu.VMEM), pl.BlockSpec(memory_space=pltpu.HBM)
    two = jax.ShapeDtypeStruct((2 * POS, HEAD_DIM), BF16)
    message = jax.ShapeDtypeStruct((2 * (POS + EDGE), HEAD_DIM), BF16)
    return pl.pallas_call(
        pack_kernel,
        out_shape=(two, message),
        in_specs=[here] * 4,
        out_specs=(vmem,) * 2,
        scratch_shapes=[pltpu.SemaphoreType.DMA((6,))],
        compiler_params=pltpu.CompilerParams(vmem_limit_bytes=8 << 20),
        name="pack",
    )(k, v, q, x)


def scale_kernel(place, k, v, q, x, weight_in, gain_in, kv, upper, scaled, weight, gain, sems):
    pairs = [(weight_in, weight), (gain_in, gain), (k, kv.at[0:POS]), (v, kv.at[POS:])]
    copies = move(pairs + message_moves(k, v, q, x, upper, slice(0, EDGE)), sems)
    for copy in copies[:2]:
        copy.wait()
    depth = weight.shape[0]
    gains = gain[...].astype(F32)
    line = lax.broadcasted_iota(jnp.int32, gains.shape, 0) == place[0]
    mine = jnp.sum(jnp.where(line, gains, 0.0), axis=0, keepdims=True)
    mine = jnp.transpose(jnp.broadcast_to(mine, (depth, depth)))
    for c in range(0, weight.shape[1], depth):
        scaled[:, c : c + depth] = (weight[:, c : c + depth].astype(F32) * mine).astype(BF16)
    for copy in copies[2:]:
        copy.wait()


def scale(place, k, v, q, x, weight, gain):
    vmem, here = pl.BlockSpec(memory_space=pltpu.VMEM), pl.BlockSpec(memory_space=pltpu.HBM)
    message = jax.ShapeDtypeStruct((2 * (POS + EDGE), HEAD_DIM), BF16)
    return pl.pallas_call(
        scale_kernel,
        out_shape=(
            jax.ShapeDtypeStruct((2 * POS, HEAD_DIM), BF16),
            message,
            jax.ShapeDtypeStruct(weight.shape, BF16),
        ),
        in_specs=[pl.BlockSpec(memory_space=pltpu.SMEM)] + [here] * 6,
        out_specs=(vmem,) * 3,
        scratch_shapes=[
            pltpu.VMEM(weight.shape, BF16),
            pltpu.VMEM(gain.shape, BF16),
            pltpu.SemaphoreType.DMA((8,)),
        ],
        compiler_params=pltpu.CompilerParams(vmem_limit_bytes=8 << 20),
        name="scale",
    )(place, k, v, q, x, weight, gain)


TALL = ROWS + 2 * MARGIN
TO_LOG2 = math.log2(math.e) / math.sqrt(HEAD_DIM)
TILE = 2 * IMG_W


def spread_rows(above, own, below, rows, at):
    rows[0:EDGE] = above[at : at + EDGE]
    rows[EDGE : EDGE + POS] = own
    rows[EDGE + POS :] = below[at : at + EDGE]


def weigh(queries, parts, peak):
    scores = [
        lax.dot_general(queries, part[0:POS], (((1,), (1,)), ((), ())), preferred_element_type=F32)
        for part in parts
    ]
    highest = jnp.max(functools.reduce(jnp.maximum, scores), axis=1, keepdims=True)
    if peak is not None:
        highest = jnp.maximum(highest, peak)
    weights = [jnp.exp2((score - highest) * TO_LOG2) for score in scores]
    total = jnp.sum(functools.reduce(jnp.add, weights), axis=1, keepdims=True)
    summed = functools.reduce(
        jnp.add,
        [
            jnp.dot(weight.astype(BF16), part[POS : 2 * POS], preferred_element_type=F32)
            for weight, part in zip(weights, parts)
        ],
    )
    return highest, total, summed


def near_kernel(kv, qx, above, below, summed_out, peak_out, total_out, qs, xs):
    spread_rows(above, qx[0:POS], below, qs, 2 * POS)
    spread_rows(above, qx[POS:], below, xs, 2 * POS + EDGE)
    for t in range(TALL // 2):
        own = slice(t * TILE, (t + 1) * TILE)
        peak, total, summed = weigh(qs[own], (kv, above, below), None)
        summed_out[own] = summed
        peak_out[own] = jnp.broadcast_to(peak, summed.shape)
        total_out[own] = jnp.broadcast_to(total, summed.shape)


def near(kv, qx, above, below):
    vmem = pl.BlockSpec(memory_space=pltpu.VMEM)
    out = jax.ShapeDtypeStruct((POS + 2 * EDGE, HEAD_DIM), F32)
    flops = 3 * (POS + 2 * EDGE) * SEQ * POS * HEAD_DIM
    return pl.pallas_call(
        near_kernel,
        out_shape=(out,) * 3 + (jax.ShapeDtypeStruct(out.shape, BF16),) * 2,
        in_specs=[vmem] * 4,
        out_specs=(vmem,) * 5,
        compiler_params=pltpu.CompilerParams(vmem_limit_bytes=16 << 20),
        cost_estimate=pl.CostEstimate(flops=flops, bytes_accessed=3 << 20, transcendentals=2 << 20),
        name="near",
    )(kv, qx, above, below)


def attend_kernel(place, far, summed_in, peak_in, total_in, qs, xs, taps, bias, res, conv, image):
    tall = TALL
    blank = jnp.zeros((tall, 8, HEAD_DIM), F32)
    image[:, 0:LEFT, :] = blank
    image[:, LEFT + IMG_W : LEFT + IMG_W + 8, :] = blank
    for t in range(tall // 2):
        own = slice(t * TILE, (t + 1) * TILE)
        before = peak_in[own]
        peak, total, summed = weigh(qs[own], (far,), before[:, 0:1])
        factor = jnp.exp2((before - peak) * TO_LOG2)
        total = total_in[own] * factor + total
        summed = summed_in[own] * factor + summed
        out = (xs[own].astype(F32) + summed / total).astype(BF16).astype(F32)
        image[2 * t : 2 * t + 2, LEFT : LEFT + IMG_W, :] = out.reshape(2, IMG_W, HEAD_DIM)

    @pl.when(place[0] == 0)
    def _():
        image[0:MARGIN] = jnp.zeros((MARGIN, IMG_W + 16, HEAD_DIM), F32)

    @pl.when(place[0] == SEQ - 1)
    def _():
        image[tall - MARGIN :] = jnp.zeros((MARGIN, IMG_W + 16, HEAD_DIM), F32)

    for i in range(ROWS):
        res[i * IMG_W : (i + 1) * IMG_W] = image[MARGIN + i, LEFT : LEFT + IMG_W, :].astype(BF16)
    wide = 16
    for c0 in range(0, IMG_W, wide):
        sums = [jnp.broadcast_to(bias[...], (wide, HEAD_DIM)) for _ in range(ROWS)]
        for b in range(KERNEL):
            start = LEFT - MARGIN + b + c0
            columns = [image[r, start : start + wide, :] for r in range(tall)]
            for a in range(KERNEL):
                tap = taps[a * KERNEL + b : a * KERNEL + b + 1, :]
                for i in range(ROWS):
                    sums[i] = sums[i] + columns[i + a] * tap
        for i in range(ROWS):
            conv[i, c0 : c0 + wide] = sums[i].astype(BF16)


def attend(place, far, begun, taps, bias):
    out = jax.ShapeDtypeStruct((POS, HEAD_DIM), BF16)
    vmem = pl.BlockSpec(memory_space=pltpu.VMEM)
    flops = (POS + 2 * EDGE) * SEQ * POS * HEAD_DIM
    return pl.pallas_call(
        attend_kernel,
        out_shape=(out, jax.ShapeDtypeStruct((ROWS, IMG_W, HEAD_DIM), BF16)),
        in_specs=[pl.BlockSpec(memory_space=pltpu.SMEM)] + [vmem] * 8,
        out_specs=(vmem, vmem),
        scratch_shapes=[
            pltpu.VMEM((TALL, IMG_W + 16, HEAD_DIM), F32),
        ],
        compiler_params=pltpu.CompilerParams(vmem_limit_bytes=16 << 20),
        cost_estimate=pl.CostEstimate(flops=flops, bytes_accessed=2 << 20, transcendentals=1 << 19),
        name="attend",
    )(place, far, *begun, taps, bias)


AUX = 16


def fetch(weights, groups, targets, sems):
    copies = []
    for n, group in enumerate(groups):
        rows = weights.shape[2]
        copies.append(
            [
                pltpu.make_async_copy(
                    weights.at[j, group], targets[n].at[j * rows : (j + 1) * rows], sems.at[n, j]
                )
                for j in range(SEQ)
            ]
        )
        for copy in copies[-1]:
            copy.start()
    return copies


def slab_scratch(count, weights):
    _, _, rows, columns = weights.shape
    return [
        pltpu.VMEM((count, SEQ * rows, columns), BF16),
        pltpu.SemaphoreType.DMA((count + 1, SEQ)),
    ]


def extra_rows(gain, offset, group):
    tiles = []
    for j in range(SEQ):
        here = pl.ds(j * CLASSES + group, 1)
        ratio = offset[here] / gain[here]
        high = ratio.astype(BF16).astype(F32)
        row = lax.broadcasted_iota(jnp.int32, (AUX, HEAD_DIM), 0)
        tile = jnp.where(row == 0, 1.0, 0.0)
        tile = jnp.where(row == 1, jnp.broadcast_to(high, tile.shape), tile)
        tile = jnp.where(row == 2, jnp.broadcast_to(ratio - high, tile.shape), tile)
        tiles.append(tile.astype(BF16))
    return jnp.concatenate(tiles, axis=1)


def product_of(blocks, copies, slab, gain, offset, group):
    left = jnp.concatenate([block[...] for block in blocks], axis=1)
    left = jnp.concatenate([left, extra_rows(gain, offset, group)], axis=0)
    for copy in copies:
        copy.wait()
    return jnp.dot(left, slab[...], preferred_element_type=F32)


def add_stats(blocks, pivot, before1, before2, sum1, sum2, rows=64):
    for t in range(0, POS, rows):
        here = slice(t, t + rows)
        centre, one, two = pivot[here], before1[here], before2[here]
        for block in blocks:
            away = block[here].astype(F32) - centre
            one = one + away
            two = two + away * away
        sum1[here] = one
        sum2[here] = two


def first_kernel(offsets, place, *refs):
    count = len(offsets)
    parts, refs = refs[:count], refs[count:]
    weights, gain, offset, acc, pivot, sum1, sum2, slabs, sems = refs
    groups = [lax.rem(place[0] + away + CLASSES, CLASSES) for away in offsets]
    copies = fetch(weights, groups, [slabs.at[n] for n in range(count)], sems)
    lead = jnp.mean(parts[0][0].astype(F32), axis=1, keepdims=True)
    pivot[...] = jnp.broadcast_to(lead, (POS, HEAD_DIM))
    sum1[...] = jnp.zeros((POS, HEAD_DIM), F32)
    sum2[...] = jnp.zeros((POS, HEAD_DIM), F32)
    for n, part in enumerate(parts):
        blocks = [part.at[j] for j in range(SEQ)]
        product = product_of(blocks, copies[n], slabs.at[n], gain, offset, groups[n])
        if n == 0:
            acc[...] = product
        else:
            acc[...] += product
        add_stats(blocks, pivot, sum1, sum2, sum1, sum2)


def more_kernel(offsets, place, *refs):
    count = len(offsets)
    parts, refs = refs[:count], refs[count:]
    acc, pivot, sum1, sum2, weights, gain, offset, *refs = refs
    acc_out, sum1_out, sum2_out, slab_out, slabs, sems = refs
    groups = [lax.rem(place[0] + away + CLASSES, CLASSES) for away in (*offsets, SEQ)]
    targets = [slabs.at[n] for n in range(count)] + [slab_out]
    copies = fetch(weights, groups, targets, sems)
    for n, part in enumerate(parts):
        blocks = [part.at[j] for j in range(SEQ)]
        before = (acc, sum1, sum2) if n == 0 else (acc_out, sum1_out, sum2_out)
        product = product_of(blocks, copies[n], slabs.at[n], gain, offset, groups[n])
        acc_out[...] = before[0][...] + product
        add_stats(blocks, pivot, before[1], before[2], sum1_out, sum2_out)
    for copy in copies[count]:
        copy.wait()


def stage(kernel, offsets, place, parts, before, weights, gain, offset):
    vmem, here = pl.BlockSpec(memory_space=pltpu.VMEM), pl.BlockSpec(memory_space=pltpu.HBM)
    hidden = weights.shape[-1]
    stat = jax.ShapeDtypeStruct((POS, HEAD_DIM), F32)
    total = jax.ShapeDtypeStruct((POS + AUX, hidden), F32)
    slab = jax.ShapeDtypeStruct((SEQ * weights.shape[2], hidden), BF16)
    out_shape = (total, stat, stat, slab) if before else (total, stat, stat, stat)
    return pl.pallas_call(
        functools.partial(kernel, offsets),
        out_shape=out_shape,
        in_specs=[pl.BlockSpec(memory_space=pltpu.SMEM)]
        + [vmem] * (len(parts) + len(before))
        + [here, vmem, vmem],
        out_specs=(vmem,) * len(out_shape),
        scratch_shapes=slab_scratch(len(parts), weights),
        compiler_params=pltpu.CompilerParams(vmem_limit_bytes=16 << 20),
        cost_estimate=pl.CostEstimate(
            flops=len(parts) << 28, bytes_accessed=len(parts) << 20, transcendentals=0
        ),
        name="stage",
    )(place, *parts, *before, weights, gain, offset)


def last_kernel(place, *refs):
    acc, pivot, sum1, sum2, part, slab, gain, offset, bias, out, one, two = refs
    group = lax.rem(place[0] + SEQ, CLASSES)
    blocks = [part.at[j] for j in range(SEQ)]
    add_stats(blocks, pivot, sum1, sum2, one, two)
    product = acc[...] + product_of(blocks, (), slab, gain, offset, group)
    mean1 = jnp.sum(one[...], axis=1, keepdims=True) * (1.0 / C)
    mean2 = jnp.sum(two[...], axis=1, keepdims=True) * (1.0 / C)
    centre = pivot[:, 0:1] + mean1
    spread = jnp.maximum(mean2 - mean1 * mean1, 0.0)
    scale = lax.rsqrt(spread + 1e-06)
    slope = product[POS : POS + 1]
    level = product[POS + 1 : POS + 2] + product[POS + 2 : POS + 3] + bias[...]
    project = scale * (product[0:POS] - centre * slope) + level
    out[...] = (0.5 * project * (1.0 + lax.erf(project * math.sqrt(0.5)))).astype(BF16)


def last(place, acc, stats, part, slab, gain, offset, bias):
    vmem = pl.BlockSpec(memory_space=pltpu.VMEM)
    return pl.pallas_call(
        last_kernel,
        out_shape=jax.ShapeDtypeStruct((POS, bias.shape[1]), BF16),
        in_specs=[pl.BlockSpec(memory_space=pltpu.SMEM)] + [vmem] * 9,
        out_specs=vmem,
        scratch_shapes=[pltpu.VMEM((POS, HEAD_DIM), F32)] * 2,
        compiler_params=pltpu.CompilerParams(vmem_limit_bytes=16 << 20),
        cost_estimate=pl.CostEstimate(flops=1 << 28, bytes_accessed=4 << 20, transcendentals=1 << 18),
        name="last",
    )(place, acc, *stats, part, slab, gain, offset, bias)


def on_device(
    inputs,
    query_proj,
    key_proj,
    value_proj,
    depth_weight,
    depth_bias,
    norm_gain,
    norm_bias,
    expand_weight,
    expand_bias,
):
    seq, row, col = (lax.axis_index(axis) for axis in ("seq", "row", "col"))
    depth, hidden = expand_weight.shape
    gain, offset = (a.reshape(C // depth, depth) for a in (norm_gain, norm_bias))
    x, q, k, v = (a.reshape(POS, HEAD_DIM) for a in (inputs, query_proj, key_proj, value_proj))
    x, q, k, v = (pltpu.with_memory_space_constraint(a, pltpu.HBM) for a in (x, q, k, v))
    mine = (seq * CLASSES + row).astype(jnp.int32).reshape(1)
    held = (pltpu.with_memory_space_constraint(a, pltpu.HBM) for a in (expand_weight, gain))
    qx, lower = pack(k, v, q, x)
    above = shift(lower, "seq", 1)
    kv, upper, scaled = scale(mine, k, v, q, x, *held)
    below, far = shift(upper, "seq", -1), shift(kv, "seq", 2)
    weights = lax.all_gather(scaled, ("seq", "row"), axis=0, tiled=True)
    weights = weights.reshape(SEQ, CLASSES, depth, hidden)
    weights = pltpu.with_memory_space_constraint(weights, pltpu.HBM)
    gain, offset = gain.astype(F32), offset.astype(F32)
    taps = depth_weight.astype(F32).reshape(KERNEL * KERNEL, HEAD_DIM)
    bias = depth_bias.astype(F32).reshape(1, HEAD_DIM)
    begun = near(kv, qx, above, below)
    residual, convolved = attend(
        seq.astype(jnp.int32).reshape(1), far, begun, taps, bias
    )

    strides = [[i + CLASSES * j for j in range(SEQ)] for i in range(CLASSES)]
    own = lax.all_gather(convolved, "col", axis=0, tiled=True, axis_index_groups=strides)
    own = own.reshape(SEQ, POS, HEAD_DIM)
    pairs, up, down = [], own, own
    for _ in range(3):
        up, down = shift(up, "col", 1), shift(down, "col", -1)
        pairs.append((up, down))
    place = col.astype(jnp.int32).reshape(1)
    parts = (own, *pairs[0], *pairs[1])
    before = stage(first_kernel, (0, -1, 1, -2, 2), place, parts, (), weights, gain, offset)
    up, before = lax.optimization_barrier((up, before))
    pairs[2] = (up, down)
    up = shift(up, "col", 1)
    acc, *sums, slab = stage(more_kernel, (-3, 3), place, pairs[2], before, weights, gain, offset)
    pivot = before[1]
    bias = expand_bias.astype(F32).reshape(1, hidden)
    out = last(place, acc, (pivot, *sums), up, slab, gain, offset, bias)
    return (
        residual.reshape(inputs.shape),
        out.reshape(inputs.shape[:3] + (hidden,)),
    )


def solution(mesh):
    return jax.shard_map(
        on_device,
        mesh=mesh,
        in_specs=(
            P("row", "seq", None, "col"),
            P("row", "seq", None, "col"),
            P("row", "seq", None, "col"),
            P("row", "seq", None, "col"),
            P(None, None, "col"),
            P("col"),
            P(),
            P(),
            P(("seq", "row"), "col"),
            P("col"),
        ),
        out_specs=(P("row", "seq", None, "col"), P("row", "seq", None, "col")),
        check_vma=False,
    )
```
